32 devices in a mesh: sample: 2 (over y), gx: 8 (over z, x), gy: 2 (over core).
Axes of the slice: x: 2, y: 2, z: 4, core: 2. Of those that a mesh axis runs over, the one named last changes fastest.
Arguments:
- body_force: float32 [3, 64, 32, 256], P(None, 'sample', 'gx', 'gy'), parts along dimension 1, may hold values from -36 to 36
- modulus: float32 [64, 32, 256], P('sample', 'gx', 'gy'), parts along dimension 0, may hold values from 0.12 to 8.2
Outputs:
- solution_field: float32 [3, 64, 32, 256], P(None, 'sample', 'gx', 'gy'), parts along dimension 1
- stress: float32 [6, 64, 32, 256], P(None, 'sample', 'gx', 'gy'), parts along dimension 1
The draws below stay inside these ranges and needn't reach their ends.
There are 2 independent parts, one for each index of `sample`. The reference program is written for one: setup_inputs(seed, part) draws one part's arguments, and reference() takes and returns one part's arrays. A program takes and returns all parts, laid end to end along the dimension named above; each array names one. Nothing has to cross between parts.
All inputs are finite; a program needn't handle non-finite values.
Results may differ from the reference program's by a relative error of at most 0.0039.
Values sent between devices are 32-bit elements; how exact they have to be, the bound alone decides.
No kernel may reach another device: no remote copies, remote signals or barrier semaphores. Data moves between devices by JAX's collectives and lax.ppermute only.
A program may use at most 64 MiB of HBM per device.

```python
import math
import jax
import jax.numpy as jnp
import numpy as np
from jax import lax

EZ = 32
ITERS = 2
NX = 32
NY = 256
N_GX = 8


def draw_body_force(key, part):
    key_noise = jax.random.fold_in(key, 11)
    key_rows = jax.random.fold_in(key, 12)
    key_cols = jax.random.fold_in(key, 13)
    x_frac = jnp.arange(NX, dtype=jnp.float32) / NX
    x_ramp = jnp.exp(jnp.log(3.0) * x_frac)
    row_scale = jnp.exp(jax.random.uniform(key_rows, (NX,), jnp.float32, 0.0, jnp.log(10.0)))
    col_scale = jnp.exp(jax.random.uniform(key_cols, (NY,), jnp.float32, 0.0, jnp.log(10.0)))
    noise = jnp.clip(jax.random.normal(key_noise, (3, EZ, NX, NY), jnp.float32), -4.0, 4.0)
    scaled = 0.03 * noise * (x_ramp * row_scale)[None, None, :, None] * col_scale[None, None, None, :]
    return scaled.astype(jnp.float32)


def draw_modulus(key, part):
    key_field = jax.random.fold_in(key, 21)
    logs = 0.7 * jnp.clip(jax.random.normal(key_field, (EZ, NX, NY), jnp.float32), -3.0, 3.0)
    return jnp.exp(logs).astype(jnp.float32)


def setup_inputs(seed: int = 0, part: int = 0) -> dict:
    keys = jax.random.split(jax.random.key(seed), 3)
    own_keys = jax.random.split(jax.random.fold_in(keys[2], part), 3)
    return {
        "body_force": draw_body_force(jax.random.fold_in(jax.random.fold_in(keys[2], part), 71), part),
        "modulus": draw_modulus(jax.random.fold_in(jax.random.fold_in(keys[2], part), 71), part),
    }


def corner_list():
    return [(off_z, off_x, off_y) for off_z in (0, 1) for off_x in (0, 1) for off_y in (0, 1)]

def strain_matrix(point):
    corners = corner_list()
    grads = np.zeros((3, 8))
    for corner, offsets in enumerate(corners):
        for axis in range(3):
            value = 1.0 if offsets[axis] else -1.0
            for other in range(3):
                if other != axis:
                    value = value * (point[other] if offsets[other] else 1.0 - point[other])
            grads[axis, corner] = value
    strain = np.zeros((6, 24))
    for corner in range(8):
        for axis in range(3):
            strain[axis, axis * 8 + corner] = grads[axis, corner]
        strain[3, 0 * 8 + corner] = grads[1, corner]
        strain[3, 1 * 8 + corner] = grads[0, corner]
        strain[4, 1 * 8 + corner] = grads[2, corner]
        strain[4, 2 * 8 + corner] = grads[1, corner]
        strain[5, 0 * 8 + corner] = grads[2, corner]
        strain[5, 2 * 8 + corner] = grads[0, corner]
    return strain

def tables():
    poisson = 0.3
    lame_first = poisson / ((1.0 + poisson) * (1.0 - 2.0 * poisson))
    shear_mod = 1.0 / (2.0 * (1.0 + poisson))
    elastic = np.zeros((6, 6))
    elastic[:3, :3] = lame_first
    for axis in range(3):
        elastic[axis, axis] += 2.0 * shear_mod
        elastic[axis + 3, axis + 3] = shear_mod
    gauss_pts = [0.5 - 0.5 / math.sqrt(3.0), 0.5 + 0.5 / math.sqrt(3.0)]
    stiffness = np.zeros((24, 24))
    for first in gauss_pts:
        for second in gauss_pts:
            for third in gauss_pts:
                strain = strain_matrix((first, second, third))
                stiffness += strain.T @ elastic @ strain / 8.0
    stress_map = elastic @ strain_matrix((0.5, 0.5, 0.5))
    return (jnp.asarray(stiffness, jnp.float32), jnp.asarray(stress_map, jnp.float32))

def element_values(padded, modulus, matrix):
    z_cells, x_cells, y_cells = modulus.shape
    pieces = [padded[channel, off_z:off_z + z_cells, off_x:off_x + x_cells, off_y:off_y + y_cells] for channel in range(3) for off_z, off_x, off_y in corner_list()]
    stacked = jnp.stack(pieces)
    result = jnp.einsum('pq,qzxy->pzxy', matrix, stacked, precision=lax.Precision.HIGHEST)
    return result * modulus

def spread(values, per_corner):
    summed = None
    for corner, (off_z, off_x, off_y) in enumerate(corner_list()):
        corner_part = values[corner::8] if per_corner else values
        placed = jnp.pad(corner_part, ((0, 0), (off_z, 1 - off_z), (off_x, 1 - off_x), (off_y, 1 - off_y)))
        summed = placed if summed is None else summed + placed
    return summed

def assemble(field_in, modulus, matrix, per_corner):
    z_cells, x_total, y_total = modulus.shape
    block_width = x_total // N_GX
    padded = jnp.pad(field_in, ((0, 0), (1, 0), (1, 0), (1, 0)))

    def block_at(block_index):
        block_start = block_index * block_width
        padded_block = lax.dynamic_slice_in_dim(padded, block_start, block_width + 1, 2)
        modulus_block = lax.dynamic_slice_in_dim(modulus, block_start, block_width, 1)
        return spread(element_values(padded_block, modulus_block, matrix), per_corner)
    blocks = lax.map(block_at, jnp.arange(N_GX, dtype=jnp.int32))
    channels = blocks.shape[1]
    main_rows = jnp.transpose(blocks[:, :, :, :block_width, :], (1, 2, 0, 3, 4))
    main_rows = main_rows.reshape(channels, z_cells + 1, x_total, y_total + 1)
    assembled = jnp.pad(main_rows, ((0, 0), (0, 0), (0, 1), (0, 0)))
    tail_rows = jnp.transpose(blocks[:, :, :, block_width, :], (1, 2, 0, 3))
    assembled = assembled.at[:, :, block_width::block_width, :].add(tail_rows)
    return assembled[:, 1:, 1:, 1:]

def node_factor(cells):
    nodes = jnp.arange(1, cells + 1, dtype=jnp.int32)
    return jnp.where(nodes < cells, jnp.float32(2.0), jnp.float32(1.0))

def reference(body_force, modulus):
    stiffness, stress_map = tables()
    z_cells, x_total, y_total = modulus.shape
    solution_field = jnp.zeros_like(body_force)
    residual = body_force
    direction = body_force
    norm_now = jnp.sum(residual * residual)
    for iteration in range(ITERS):
        image_vec = assemble(direction, modulus, stiffness, True)
        step_len = norm_now / jnp.sum(direction * image_vec)
        solution_field = solution_field + step_len * direction
        residual = residual - step_len * image_vec
        norm_next = jnp.sum(residual * residual)
        direction = residual + norm_next / norm_now * direction
        norm_now = norm_next
    summed = assemble(solution_field, modulus, stress_map, False)
    counts = node_factor(z_cells)[:, None, None] * node_factor(x_total)[None, :, None] * node_factor(y_total)[None, None, :]
    stress = summed / counts
    return (solution_field, stress)
```

```python
import functools

import jax
import jax.numpy as jnp
from jax import lax
from jax.experimental import pallas as pl
from jax.experimental.pallas import tpu as pltpu
from jax.sharding import PartitionSpec as P

POISSON = 0.3
LAME = POISSON / ((1.0 + POISSON) * (1.0 - 2.0 * POISSON))
SHEAR = 1.0 / (2.0 * (1.0 + POISSON))
RATIO = LAME / SHEAR
ONE = SHEAR / 16.0
TWO = SHEAR / 48.0
THREE = (LAME + 4.0 * SHEAR) / 144.0

VMEM = pl.BlockSpec(memory_space=pltpu.VMEM)
LIMIT = pltpu.CompilerParams(vmem_limit_bytes=48 << 20)


def lanes(shape):
    return lax.broadcasted_iota(jnp.int32, shape, len(shape) - 1)


def from_left(first, second):
    edge = lanes(first.shape) == 0
    turned, turned2 = pltpu.roll(first, 1, 1), pltpu.roll(second, 1, 1)
    return jnp.where(edge, 0.0, turned), jnp.where(edge, turned, turned2)


def from_right(first, second):
    edge = lanes(first.shape) == first.shape[1] - 1
    turned, turned2 = (pltpu.roll(v, v.shape[1] - 1, 1) for v in (first, second))
    return jnp.where(edge, turned2, turned), jnp.where(edge, 0.0, turned2)


def pack_kernel(force_ref, modulus_ref, own_ref, same_ref, cross_ref):
    core = lax.axis_index("gy")
    cells = own_ref.shape[2]

    def plane(field, x):
        rows = pl.ds(x, cells, stride=4)
        return force_ref[field, rows, :] if field < 3 else modulus_ref[rows, :]

    for field in range(4):
        for x in range(4):
            own_ref[x, field] = plane(field, x)
        for i in range(2):
            same_ref[i, field] = plane(field, 2 * (1 - core) + i)
            cross_ref[i, field] = plane(field, 2 * core + i)


def gather_planes(own_ref, mate_ref, same_ref, cross_ref, node_ref, elem_ref):
    core = lax.axis_index("gy")
    cells = own_ref.shape[2]
    node_ref[:, :, :, 0:8, :] = jnp.zeros((6, 3, 2, 8, own_ref.shape[3]), jnp.float32)
    for x in range(4):
        at = 2 * (1 - core) + x
        for ref, block in ((own_ref, core), (mate_ref, 1 - core)):
            for field in range(3):
                node_ref[at, field, block, 8 : 8 + cells, :] = ref[x, field]
            elem_ref[at, block] = ref[x, 3]
    for x in range(2):
        at = 4 * core + x
        for ref, block in ((same_ref, core), (cross_ref, 1 - core)):
            for field in range(3):
                node_ref[at, field, block, 8 : 8 + cells, :] = ref[x, field]
            elem_ref[at, block] = ref[x, 3]


def plane_modes(read, cells):
    sums, diffs = [], []
    for block in range(2):
        high, low = read(block, 8, cells), read(block, 7, cells)
        sums.append(high + low)
        diffs.append(high - low)
    sums_left, diffs_left = from_left(*sums), from_left(*diffs)
    out = []
    for block in range(2):
        s, d, sl, dl = sums[block], diffs[block], sums_left[block], diffs_left[block]
        out.append((s + sl, d + dl, s - sl, d - dl))
    return out


def element_modes(low, high):
    found = []
    for component in range(3):
        modes = {}
        for kind, (z, y) in enumerate(((0, 0), (1, 0), (0, 1), (1, 1))):
            lo, hi = low[component][kind], high[component][kind]
            if (z, y) != (0, 0):
                modes[z, 0, y] = hi + lo
            modes[z, 1, y] = hi - lo
        found.append(modes)
    return found


def mode_forces(modes, modulus):
    u, v, w = modes
    one, two, three = modulus * ONE, modulus * TWO, modulus * THREE
    trace = RATIO * (u[1, 0, 0] + v[0, 1, 0] + w[0, 0, 1])
    shear_zx = one * (u[0, 1, 0] + v[1, 0, 0])
    shear_xy = one * (v[0, 0, 1] + w[0, 1, 0])
    shear_zy = one * (u[0, 0, 1] + w[1, 0, 0])
    trace_z = RATIO * (v[1, 1, 0] + w[1, 0, 1])
    trace_x = RATIO * (u[1, 1, 0] + w[0, 1, 1])
    trace_y = RATIO * (u[1, 0, 1] + v[0, 1, 1])
    mixed_zx = u[0, 1, 1] + v[1, 0, 1]
    mixed_xy = v[1, 0, 1] + w[1, 1, 0]
    mixed_zy = u[0, 1, 1] + w[1, 1, 0]
    return (
        {
            (1, 0, 0): one * (trace + 2.0 * u[1, 0, 0]),
            (0, 1, 0): shear_zx,
            (0, 0, 1): shear_zy,
            (1, 1, 0): two * (trace_x + 3.0 * u[1, 1, 0]),
            (1, 0, 1): two * (trace_y + 3.0 * u[1, 0, 1]),
            (0, 1, 1): two * (mixed_zx + mixed_zy),
            (1, 1, 1): three * u[1, 1, 1],
        },
        {
            (0, 1, 0): one * (trace + 2.0 * v[0, 1, 0]),
            (1, 0, 0): shear_zx,
            (0, 0, 1): shear_xy,
            (1, 1, 0): two * (trace_z + 3.0 * v[1, 1, 0]),
            (0, 1, 1): two * (trace_y + 3.0 * v[0, 1, 1]),
            (1, 0, 1): two * (mixed_zx + mixed_xy),
            (1, 1, 1): three * v[1, 1, 1],
        },
        {
            (0, 0, 1): one * (trace + 2.0 * w[0, 0, 1]),
            (1, 0, 0): shear_zy,
            (0, 1, 0): shear_xy,
            (1, 0, 1): two * (trace_z + 3.0 * w[1, 0, 1]),
            (0, 1, 1): two * (trace_x + 3.0 * w[0, 1, 1]),
            (1, 1, 0): two * (mixed_xy + mixed_zy),
            (1, 1, 1): three * w[1, 1, 1],
        },
    )


def mode_energy(modes, modulus):
    u, v, w = modes
    square = lambda value: value * value
    a, b, c = u[1, 0, 0], v[0, 1, 0], w[0, 0, 1]
    one = RATIO * square(a + b + c) + 2.0 * (square(a) + square(b) + square(c))
    one = one + square(u[0, 1, 0] + v[1, 0, 0]) + square(v[0, 0, 1] + w[0, 1, 0]) + square(u[0, 0, 1] + w[1, 0, 0])
    d, e, f = u[1, 1, 0], u[1, 0, 1], v[1, 1, 0]
    g, h, k = v[0, 1, 1], w[1, 0, 1], w[0, 1, 1]
    two = RATIO * (square(f + h) + square(d + k) + square(e + g))
    two = two + 3.0 * (square(d) + square(e) + square(f) + square(g) + square(h) + square(k))
    m, n, o = u[0, 1, 1], v[1, 0, 1], w[1, 1, 0]
    two = two + square(m + n) + square(n + o) + square(m + o)
    three = square(u[1, 1, 1]) + square(v[1, 1, 1]) + square(w[1, 1, 1])
    return modulus * (ONE * one + TWO * two + THREE * three)


def spread_kernel(own_ref, mate_ref, same_ref, cross_ref, image_ref, sums_ref, node_ref, elem_ref, mode_ref, part_ref):
    core, slab = lax.axis_index("gy"), lax.axis_index("gx")
    cells, width = own_ref.shape[2:]
    tiles = cells // 8
    gather_planes(own_ref, mate_ref, same_ref, cross_ref, node_ref, elem_ref)

    @pl.loop(0, 6)
    def _(j):
        for field in range(3):
            read = lambda block, start, size: node_ref[j, field, block, start : start + size, :]
            for block, kinds in enumerate(plane_modes(read, cells)):
                for kind, value in enumerate(kinds):
                    mode_ref[j, 4 * field + kind, block] = value

    part_ref[:, :, :, cells : cells + 8, :] = jnp.zeros((4, 12, 2, 8, width), jnp.float32)

    @pl.loop(0, 2 * tiles)
    def _(t):
        block, rows = t // tiles, pl.ds(pl.multiple_of((t % tiles) * 8, 8), 8)
        load = lambda j: [[mode_ref[j, 4 * f + k, block, rows, :] for k in range(4)] for f in range(3)]
        low, kept = load(0), None
        for j in range(1, 6):
            high = load(j)
            forces = mode_forces(element_modes(low, high), elem_ref[j, block, rows, :])
            after = []
            for f in range(3):
                upper, lower = [], []
                for z, y in ((0, 0), (1, 0), (0, 1), (1, 1)):
                    diff, both = forces[f][z, 1, y], forces[f].get((z, 0, y))
                    upper.append(diff if both is None else both + diff)
                    lower.append(-diff if both is None else both - diff)
                after.append(upper)
                if kept is not None:
                    ss, ds, sd, dd = (p + q for p, q in zip(kept[f], lower))
                    here, back = ss + ds, ss - ds
                    here_y, back_y = sd + dd, sd - dd
                    part_ref[j - 2, 4 * f, block, rows, :] = here + here_y
                    part_ref[j - 2, 4 * f + 1, block, rows, :] = here - here_y
                    part_ref[j - 2, 4 * f + 2, block, rows, :] = back + back_y
                    part_ref[j - 2, 4 * f + 3, block, rows, :] = back - back_y
            low, kept = high, after

    image_ref[:, :, :, 0:8, :] = jnp.zeros((4, 3, 2, 8, width), jnp.float32)
    clamped = jnp.where((core == 0) & (slab == 0), 0.0, 1.0)
    fold = lambda value: value.reshape(tiles, 8, width).sum(0)
    zero = jnp.zeros((8, width), jnp.float32)
    norm, cross, square = zero, zero, zero
    for j in range(4):
        for f in range(3):
            here = lambda k, block: part_ref[j, 4 * f + k, block, 0:cells, :]
            above = lambda k, block: part_ref[j, 4 * f + k, block, 1 : cells + 1, :]
            beside = from_right(*(here(1, block) + above(3, block) for block in range(2)))
            for block in range(2):
                value = here(0, block) + above(2, block) + beside[block]
                if j == 0:
                    value = value * clamped
                image_ref[j, f, block, 8 : 8 + cells, :] = value
                if j in (1, 2):
                    force = node_ref[j + 1, f, block, 8 : 8 + cells, :]
                    norm = norm + fold(force * force)
                    cross = cross + fold(force * value)
                    square = square + fold(value * value)

    @pl.loop(0, 3)
    def _(j):
        for field in range(3):
            read = lambda block, start, size: image_ref[j, field, block, start : start + size, :]
            for block, kinds in enumerate(plane_modes(read, cells)):
                for kind, value in enumerate(kinds):
                    mode_ref[j, 4 * field + kind, block] = value

    def energy_of(t, total):
        block, rows = t // tiles, pl.ds(pl.multiple_of((t % tiles) * 8, 8), 8)
        load = lambda j: [[mode_ref[j, 4 * f + k, block, rows, :] for k in range(4)] for f in range(3)]
        low = load(0)
        for j in range(1, 3):
            high = load(j)
            total = total + mode_energy(element_modes(low, high), elem_ref[j + 1, block, rows, :])
            low = high
        return total

    energy = lax.fori_loop(0, 2 * tiles, energy_of, zero)
    row = lax.broadcasted_iota(jnp.int32, (8, width), 0)
    packed = zero
    for k, value in enumerate((norm, cross, square, energy)):
        packed = jnp.where(row == k, jnp.sum(value, axis=0, keepdims=True), packed)
    sums_ref[...] = jnp.broadcast_to(packed[None], sums_ref.shape)


def stress_kernel(own_ref, mate_ref, same_ref, cross_ref, image_ref, keep_ref, send_ref, node_ref, elem_ref, mode_ref, part_ref):
    core, slab = lax.axis_index("gy"), lax.axis_index("gx")
    last = (core == 1) & (slab == lax.axis_size("gx") - 1)
    cells, width = own_ref.shape[2:]
    tiles = cells // 8
    gather_planes(own_ref, mate_ref, same_ref, cross_ref, node_ref, elem_ref)
    part_ref[:, :, :, cells : cells + 8, :] = jnp.zeros((2, 6, 2, 8, width), jnp.float32)
    row = lax.broadcasted_iota(jnp.int32, (cells, width), 0)
    lane = lanes((cells, width))

    for which in range(2):

        @pl.loop(0, 4)
        def _(j):
            for field in range(3):
                if which == 0:
                    read = lambda block, start, size: node_ref[j + 1, field, block, start : start + size, :]
                else:
                    read = lambda block, start, size: image_ref[j, field, block, start : start + size, :]
                for block, kinds in enumerate(plane_modes(read, cells)):
                    for kind in range(3):
                        mode_ref[j, 3 * field + kind, block] = kinds[kind]

        @pl.loop(0, 2 * tiles)
        def _(t):
            block, rows = t // tiles, pl.ds(pl.multiple_of((t % tiles) * 8, 8), 8)
            load = lambda j: [[mode_ref[j, 3 * f + k, block, rows, :] for k in range(3)] for f in range(3)]
            low, kept = load(0), None
            for j in range(1, 4):
                high = load(j)
                by_z = [high[f][1] + low[f][1] for f in range(3)]
                by_x = [high[f][0] - low[f][0] for f in range(3)]
                by_y = [high[f][2] + low[f][2] for f in range(3)]
                scaled = elem_ref[j + 1, block, rows, :] * (0.25 * SHEAR)
                trace = RATIO * (by_z[0] + by_x[1] + by_y[2])
                now = [
                    scaled * (trace + 2.0 * by_z[0]),
                    scaled * (trace + 2.0 * by_x[1]),
                    scaled * (trace + 2.0 * by_y[2]),
                    scaled * (by_x[0] + by_z[1]),
                    scaled * (by_y[1] + by_x[2]),
                    scaled * (by_y[0] + by_z[2]),
                ]
                if kept is not None:
                    for k in range(6):
                        part_ref[j - 2, k, block, rows, :] = kept[k] + now[k]
                low, kept = high, now

        for i in range(2):
            count_x = jnp.where(last, 1.0, 0.5) if i == 1 else 0.5
            count_z = jnp.where(row == cells - 1, 1.0, 0.5) * count_x
            counts = (count_z * 0.5, count_z * jnp.where(lane == width - 1, 1.0, 0.5))
            for k in range(6):
                both = [part_ref[i, k, block, 0:cells, :] + part_ref[i, k, block, 1 : cells + 1, :] for block in range(2)]
                beside = from_right(*both)
                values = [(both[block] + beside[block]) * counts[block] for block in range(2)]
                keep_ref[i, 6 * which + k] = jnp.where(core == 0, values[0], values[1])
                send_ref[i, 6 * which + k] = jnp.where(core == 0, values[1], values[0])
    for i in range(2):
        for f in range(3):
            keep_ref[i, 12 + f] = image_ref[i + 1, f, core, 8 : 8 + cells, :]
            send_ref[i, 12 + f] = image_ref[i + 1, f, 1 - core, 8 : 8 + cells, :]


def combine_kernel(sums_ref, own_ref, keep_ref, mate_ref, field_ref, stress_ref):
    core = lax.axis_index("gy")
    cells = own_ref.shape[2]
    total = jnp.sum(jnp.sum(sums_ref[...], axis=0), axis=1, keepdims=True)
    norm, cross, square, energy = (total[k : k + 1, :] for k in range(4))
    first = norm / cross
    norm_next = norm - 2.0 * first * cross + first * first * square
    ratio = norm_next / norm
    grown = 1.0 + ratio
    curvature = grown * grown * cross - 2.0 * grown * first * square + first * first * energy
    second = norm_next / curvature
    weight = first + second * grown
    weight_image = -second * first
    shape = (cells, own_ref.shape[3])
    weight = jnp.broadcast_to(weight, shape)
    weight_image = jnp.broadcast_to(weight_image, shape)
    for ref, base in ((keep_ref, 2 * core), (mate_ref, 2 * (1 - core))):
        for i in range(2):
            rows = pl.ds(base + i, cells, stride=4)
            for f in range(3):
                field_ref[f, rows, :] = weight * own_ref[base + i, f] + weight_image * ref[i, 12 + f]
            for k in range(6):
                stress_ref[k, rows, :] = weight * ref[i, k] + weight_image * ref[i, 6 + k]


def per_device(body_force, modulus):
    cells, planes, width = modulus.shape
    slabs, cores = lax.axis_size("gx"), lax.axis_size("gy")
    assert planes == 4 and cores == 2 and cells % 8 == 0
    both = ("gx", "gy")
    f32 = jnp.float32
    shape = lambda *dims: jax.ShapeDtypeStruct(dims, f32)

    own, same, cross = pl.pallas_call(
        pack_kernel,
        out_shape=(shape(4, 4, cells, width), shape(2, 4, cells, width), shape(2, 4, cells, width)),
        in_specs=[VMEM] * 2,
        out_specs=[VMEM] * 3,
        compiler_params=LIMIT,
        name="pack",
    )(body_force.reshape(3, cells * 4, width), modulus.reshape(cells * 4, width))

    up = [(2 * g, 2 * g + 2) for g in range(slabs - 1)]
    down = [(2 * g + 3, 2 * g + 1) for g in range(slabs - 1)]
    pairs = [(2 * g + 1, 2 * g + 2) for g in range(slabs - 1)]
    mate = lax.ppermute(own, "gy", [(0, 1), (1, 0)])
    cross_in = lax.ppermute(cross, both, pairs + [(q, p) for p, q in pairs])
    same_in = lax.ppermute(same, both, up + down)
    slabs_in = (own, mate, same_in, cross_in)

    node = pltpu.VMEM((6, 3, 2, cells + 8, width), f32)
    elem = pltpu.VMEM((6, 2, cells, width), f32)
    image, sums = pl.pallas_call(
        spread_kernel,
        out_shape=(shape(4, 3, 2, cells + 8, width), shape(slabs * cores, 8, width)),
        in_specs=[VMEM] * 4,
        out_specs=[VMEM] * 2,
        scratch_shapes=[
            node,
            elem,
            pltpu.VMEM((6, 12, 2, cells, width), f32),
            pltpu.VMEM((4, 12, 2, cells + 8, width), f32),
        ],
        compiler_params=LIMIT,
        name="spread",
    )(*slabs_in)

    sums = lax.all_to_all(sums, both, 0, 0)
    keep, send = pl.pallas_call(
        stress_kernel,
        out_shape=(shape(2, 15, cells, width), shape(2, 15, cells, width)),
        in_specs=[VMEM] * 5,
        out_specs=[VMEM] * 2,
        scratch_shapes=[
            node,
            elem,
            pltpu.VMEM((4, 9, 2, cells, width), f32),
            pltpu.VMEM((2, 6, 2, cells + 8, width), f32),
        ],
        compiler_params=LIMIT,
        cost_estimate=pl.CostEstimate(flops=10_000_000, bytes_accessed=3_000_000, transcendentals=0),
        name="stress",
    )(*slabs_in, image)
    received = lax.ppermute(send, "gy", [(0, 1), (1, 0)])

    field, stress = pl.pallas_call(
        combine_kernel,
        out_shape=(shape(3, cells * 4, width), shape(6, cells * 4, width)),
        in_specs=[VMEM] * 4,
        out_specs=[VMEM] * 2,
        compiler_params=LIMIT,
        name="combine",
    )(sums, own, keep, received)
    return field.reshape(3, cells, 4, width), stress.reshape(6, cells, 4, width)


def solution(mesh):
    return jax.shard_map(
        per_device,
        mesh=mesh,
        in_specs=(P(None, "sample", "gx", "gy"), P("sample", "gx", "gy")),
        out_specs=(P(None, "sample", "gx", "gy"), P(None, "sample", "gx", "gy")),
        check_vma=False,
    )
```

```python
import functools

import jax
import jax.numpy as jnp
from jax import lax
from jax.experimental import pallas as pl
from jax.experimental.pallas import tpu as pltpu
from jax.sharding import PartitionSpec as P

POISSON = 0.3
LAME = POISSON / ((1.0 + POISSON) * (1.0 - 2.0 * POISSON))
SHEAR = 1.0 / (2.0 * (1.0 + POISSON))
RATIO = LAME / SHEAR
ONE = SHEAR / 16.0
TWO = SHEAR / 48.0
THREE = (LAME + 4.0 * SHEAR) / 144.0

VMEM = pl.BlockSpec(memory_space=pltpu.VMEM)
LIMIT = pltpu.CompilerParams(vmem_limit_bytes=48 << 20)


def lanes(shape):
    return lax.broadcasted_iota(jnp.int32, shape, len(shape) - 1)


def from_left(first, second):
    edge = lanes(first.shape) == 0
    turned, turned2 = pltpu.roll(first, 1, 1), pltpu.roll(second, 1, 1)
    return jnp.where(edge, 0.0, turned), jnp.where(edge, turned, turned2)


def from_right(first, second):
    edge = lanes(first.shape) == first.shape[1] - 1
    turned, turned2 = (pltpu.roll(v, v.shape[1] - 1, 1) for v in (first, second))
    return jnp.where(edge, turned2, turned), jnp.where(edge, 0.0, turned2)


def pack_kernel(force_hbm, modulus_hbm, force_ref, own_ref, same_ref, cross_ref, modulus_ref, sem):
    core = lax.axis_index("gy")
    cells = own_ref.shape[2]
    copies = [
        pltpu.make_async_copy(force_hbm, force_ref, sem.at[0]),
        pltpu.make_async_copy(modulus_hbm, modulus_ref, sem.at[1]),
    ]
    for copy in copies:
        copy.start()
    for copy in copies:
        copy.wait()

    def plane(field, x):
        rows = pl.ds(x, cells, stride=4)
        return force_ref[field, rows, :] if field < 3 else modulus_ref[rows, :]

    for field in range(4):
        for x in range(4):
            own_ref[x, field] = plane(field, x)
        for i in range(2):
            same_ref[i, field] = plane(field, 2 * (1 - core) + i)
            cross_ref[i, field] = plane(field, 2 * core + i)


def plane_modes(read, cells):
    sums, diffs = [], []
    for block in range(2):
        high, low = read(block, 8, cells), read(block, 7, cells)
        sums.append(high + low)
        diffs.append(high - low)
    sums_left, diffs_left = from_left(*sums), from_left(*diffs)
    out = []
    for block in range(2):
        s, d, sl, dl = sums[block], diffs[block], sums_left[block], diffs_left[block]
        out.append((s + sl, d + dl, s - sl, d - dl))
    return out


def element_modes(low, high):
    found = []
    for component in range(3):
        modes = {}
        for kind, (z, y) in enumerate(((0, 0), (1, 0), (0, 1), (1, 1))):
            lo, hi = low[component][kind], high[component][kind]
            if (z, y) != (0, 0):
                modes[z, 0, y] = hi + lo
            modes[z, 1, y] = hi - lo
        found.append(modes)
    return found


def mode_forces(modes, modulus):
    u, v, w = modes
    one, two, three = modulus * ONE, modulus * TWO, modulus * THREE
    trace = RATIO * (u[1, 0, 0] + v[0, 1, 0] + w[0, 0, 1])
    shear_zx = one * (u[0, 1, 0] + v[1, 0, 0])
    shear_xy = one * (v[0, 0, 1] + w[0, 1, 0])
    shear_zy = one * (u[0, 0, 1] + w[1, 0, 0])
    trace_z = RATIO * (v[1, 1, 0] + w[1, 0, 1])
    trace_x = RATIO * (u[1, 1, 0] + w[0, 1, 1])
    trace_y = RATIO * (u[1, 0, 1] + v[0, 1, 1])
    mixed_zx = u[0, 1, 1] + v[1, 0, 1]
    mixed_xy = v[1, 0, 1] + w[1, 1, 0]
    mixed_zy = u[0, 1, 1] + w[1, 1, 0]
    return (
        {
            (1, 0, 0): one * (trace + 2.0 * u[1, 0, 0]),
            (0, 1, 0): shear_zx,
            (0, 0, 1): shear_zy,
            (1, 1, 0): two * (trace_x + 3.0 * u[1, 1, 0]),
            (1, 0, 1): two * (trace_y + 3.0 * u[1, 0, 1]),
            (0, 1, 1): two * (mixed_zx + mixed_zy),
            (1, 1, 1): three * u[1, 1, 1],
        },
        {
            (0, 1, 0): one * (trace + 2.0 * v[0, 1, 0]),
            (1, 0, 0): shear_zx,
            (0, 0, 1): shear_xy,
            (1, 1, 0): two * (trace_z + 3.0 * v[1, 1, 0]),
            (0, 1, 1): two * (trace_y + 3.0 * v[0, 1, 1]),
            (1, 0, 1): two * (mixed_zx + mixed_xy),
            (1, 1, 1): three * v[1, 1, 1],
        },
        {
            (0, 0, 1): one * (trace + 2.0 * w[0, 0, 1]),
            (1, 0, 0): shear_zy,
            (0, 1, 0): shear_xy,
            (1, 0, 1): two * (trace_z + 3.0 * w[1, 0, 1]),
            (0, 1, 1): two * (trace_x + 3.0 * w[0, 1, 1]),
            (1, 1, 0): two * (mixed_xy + mixed_zy),
            (1, 1, 1): three * w[1, 1, 1],
        },
    )


def mode_energy(modes, modulus):
    u, v, w = modes
    square = lambda value: value * value
    a, b, c = u[1, 0, 0], v[0, 1, 0], w[0, 0, 1]
    one = RATIO * square(a + b + c) + 2.0 * (square(a) + square(b) + square(c))
    one = one + square(u[0, 1, 0] + v[1, 0, 0]) + square(v[0, 0, 1] + w[0, 1, 0]) + square(u[0, 0, 1] + w[1, 0, 0])
    d, e, f = u[1, 1, 0], u[1, 0, 1], v[1, 1, 0]
    g, h, k = v[0, 1, 1], w[1, 0, 1], w[0, 1, 1]
    two = RATIO * (square(f + h) + square(d + k) + square(e + g))
    two = two + 3.0 * (square(d) + square(e) + square(f) + square(g) + square(h) + square(k))
    m, n, o = u[0, 1, 1], v[1, 0, 1], w[1, 1, 0]
    two = two + square(m + n) + square(n + o) + square(m + o)
    three = square(u[1, 1, 1]) + square(v[1, 1, 1]) + square(w[1, 1, 1])
    return modulus * (ONE * one + TWO * two + THREE * three)


def store_modes(mode_ref, at, field, kinds, read, cells):
    for block, found in enumerate(plane_modes(read, cells)):
        for kind in range(kinds):
            mode_ref[at, kinds * field + kind, block] = found[kind]


def face_forces(forces):
    upper, lower = [], []
    for component in range(3):
        up, down = [], []
        for z, y in ((0, 0), (1, 0), (0, 1), (1, 1)):
            diff, both = forces[component][z, 1, y], forces[component].get((z, 0, y))
            up.append(diff if both is None else both + diff)
            down.append(-diff if both is None else both - diff)
        upper.append(up)
        lower.append(down)
    return upper, lower


def corner_forces(modes):
    ss, ds, sd, dd = modes
    here, back = ss + ds, ss - ds
    here_y, back_y = sd + dd, sd - dd
    return here + here_y, here - here_y, back + back_y, back - back_y


def plus(first, second):
    return [[p + q for p, q in zip(a, b)] for a, b in zip(first, second)]


def assembled(part_ref, at, field, cells):
    here = lambda k, block: part_ref[at, 4 * field + k, block, 0:cells, :]
    above = lambda k, block: part_ref[at, 4 * field + k, block, 1 : cells + 1, :]
    beside = from_right(*(here(1, block) + above(3, block) for block in range(2)))
    return [here(0, block) + above(2, block) + beside[block] for block in range(2)]


def inner_kernel(own_ref, mate_ref, node_ref, elem_ref, image_ref, edge_mode_ref, edge_part_ref, sums_ref, mode_ref, part_ref):
    core = lax.axis_index("gy")
    cells, width = own_ref.shape[2:]
    tiles = cells // 8
    zeros = lambda *dims: jnp.zeros(dims, jnp.float32)
    node_ref[:, :, :, 0:8, :] = zeros(4, 3, 2, 8, width)
    for x in range(4):
        for ref, block in ((own_ref, core), (mate_ref, 1 - core)):
            for field in range(3):
                node_ref[x, field, block, 8 : 8 + cells, :] = ref[x, field]
            elem_ref[x, block] = ref[x, 3]

    @pl.loop(0, 4)
    def _(x):
        for field in range(3):
            read = lambda block, start, size: node_ref[x, field, block, start : start + size, :]
            store_modes(mode_ref, x, field, 4, read, cells)

    edge_mode_ref[...] = mode_ref[3 * core]
    part_ref[:, :, :, cells : cells + 8, :] = zeros(2, 12, 2, 8, width)

    @pl.loop(0, 2 * tiles)
    def _(t):
        block, rows = t // tiles, pl.ds(pl.multiple_of((t % tiles) * 8, 8), 8)
        load = lambda x: [[mode_ref[x, 4 * f + k, block, rows, :] for k in range(4)] for f in range(3)]
        low, kept, outer = load(0), None, None
        for x in range(1, 4):
            high = load(x)
            upper, lower = face_forces(mode_forces(element_modes(low, high), elem_ref[x, block, rows, :]))
            if kept is None:
                outer = lower
            else:
                for f, modes in enumerate(plus(kept, lower)):
                    for k, value in enumerate(corner_forces(modes)):
                        part_ref[x - 2, 4 * f + k, block, rows, :] = value
            low, kept = high, upper
        for f in range(3):
            for k in range(4):
                edge_part_ref[4 * f + k, block, rows, :] = jnp.where(core == 0, outer[f][k], kept[f][k])

    fold = lambda value: value.reshape(tiles, 8, width).sum(0)
    norm = cross = square = zeros(8, width)
    for i in range(2):
        mine = jnp.where(core == i, 1.0, 0.0)
        for f in range(3):
            for block, value in enumerate(assembled(part_ref, i, f, cells)):
                image_ref[i, f, block] = value
                force = node_ref[i + 1, f, block, 8 : 8 + cells, :]
                norm = norm + mine * fold(force * force)
                cross = cross + mine * fold(force * value)
                square = square + mine * fold(value * value)
    for k, value in enumerate((norm, cross, square)):
        sums_ref[k] = value


def outer_kernel(
    node_ref, elem_ref, image_ref, edge_mode_ref, edge_part_ref, part_sums_ref, same_ref, cross_ref,
    give_ref, sums_ref, halo_ref, halo_elem_ref, mode_ref, part_ref, image_mode_ref,
):
    core, slab = lax.axis_index("gy"), lax.axis_index("gx")
    cells, width = same_ref.shape[2:]
    tiles = cells // 8
    zeros = lambda *dims: jnp.zeros(dims, jnp.float32)
    near = 1 - core
    halo_ref[:, :, :, 0:8, :] = zeros(2, 3, 2, 8, width)
    for i in range(2):
        for ref, block in ((same_ref, core), (cross_ref, 1 - core)):
            for field in range(3):
                halo_ref[i, field, block, 8 : 8 + cells, :] = ref[i, field]
            halo_elem_ref[i, block] = ref[i, 3]

    mode_ref[2 * near] = edge_mode_ref[...]

    @pl.loop(0, 2)
    def _(i):
        for field in range(3):
            read = lambda block, start, size: halo_ref[i, field, block, start : start + size, :]
            store_modes(mode_ref, core + i, field, 4, read, cells)

    part_ref[:, :, :, cells : cells + 8, :] = zeros(2, 12, 2, 8, width)

    @pl.loop(0, 2 * tiles)
    def _(t):
        block, rows = t // tiles, pl.ds(pl.multiple_of((t % tiles) * 8, 8), 8)
        load = lambda x: [[mode_ref[x, 4 * f + k, block, rows, :] for k in range(4)] for f in range(3)]
        planes = [load(x) for x in range(3)]
        first = jnp.where(core == 0, halo_elem_ref[1, block, rows, :], halo_elem_ref[0, block, rows, :])
        second = jnp.where(core == 0, elem_ref[0, block, rows, :], halo_elem_ref[1, block, rows, :])
        upper, lower = face_forces(mode_forces(element_modes(planes[0], planes[1]), first))
        upper2, lower2 = face_forces(mode_forces(element_modes(planes[1], planes[2]), second))
        for f, modes in enumerate(plus(upper, lower2)):
            for k, value in enumerate(corner_forces(modes)):
                part_ref[0, 4 * f + k, block, rows, :] = value
        for f in range(3):
            modes = [
                edge_part_ref[4 * f + k, block, rows, :] + jnp.where(core == 0, upper2[f][k], lower[f][k]) for k in range(4)
            ]
            for k, value in enumerate(corner_forces(modes)):
                part_ref[1, 4 * f + k, block, rows, :] = value

    clamped = jnp.where((core == 0) & (slab == 0), 0.0, 1.0)
    fold = lambda value: value.reshape(tiles, 8, width).sum(0)
    norm, cross, square = (part_sums_ref[k] for k in range(3))
    row = lax.broadcasted_iota(jnp.int32, (cells, width), 0)
    below = lambda value: jnp.where(row == 0, 0.0, pltpu.roll(value, 1, 0))
    for f in range(3):
        value = assembled(part_ref, 0, f, cells)
        for block in range(2):
            give_ref[f, block] = value[block] * clamped
            give_ref[6 + f, block] = halo_ref[near, f, block, 8 : 8 + cells, :]
        for block, value in enumerate(assembled(part_ref, 1, f, cells)):
            give_ref[3 + f, block] = value
            force = node_ref[3 * core, f, block, 8 : 8 + cells, :]
            norm = norm + fold(force * force)
            cross = cross + fold(force * value)
            square = square + fold(value * value)
    for block in range(2):
        give_ref[9, block] = halo_elem_ref[near, block]

    @pl.loop(0, 3)
    def _(i):
        for field in range(3):
            def read(block, start, size):
                inner = image_ref[jnp.where(core == 0, 0, jnp.minimum(i, 1)), field, block]
                outer = give_ref[jnp.where(core == 0, 3 * jnp.minimum(i, 1), 3) + field, block]
                value = jnp.where((i == 2) == (core == 0), inner, outer)
                return value if start == 8 else below(value)
            store_modes(image_mode_ref, i, field, 4, read, cells)

    def energy_of(t, total):
        block, rows = t // tiles, pl.ds(pl.multiple_of((t % tiles) * 8, 8), 8)
        load = lambda x: [[image_mode_ref[x, 4 * f + k, block, rows, :] for k in range(4)] for f in range(3)]
        low = load(0)
        for x in range(2):
            high = load(x + 1)
            total = total + mode_energy(element_modes(low, high), elem_ref[2 * core + x, block, rows, :])
            low = high
        return total

    energy = lax.fori_loop(0, 2 * tiles, energy_of, zeros(8, width))
    line = lax.broadcasted_iota(jnp.int32, (8, width), 0)
    packed = zeros(8, width)
    for k, value in enumerate((norm, cross, square, energy)):
        packed = jnp.where(line == k, jnp.sum(value, axis=0, keepdims=True), packed)
    sums_ref[...] = jnp.broadcast_to(packed[None], sums_ref.shape)


def stress_kernel(
    node_ref, elem_ref, image_ref, give_ref, take_ref, basis_ref, plane_ref, outer_elem_ref, mode_ref, part_ref,
):
    core, slab = lax.axis_index("gy"), lax.axis_index("gx")
    last = slab == lax.axis_size("gx") - 1
    cells, width = elem_ref.shape[2:]
    tiles = cells // 8
    row = lax.broadcasted_iota(jnp.int32, (cells, width), 0)
    lane = lanes((cells, width))
    below = lambda value: jnp.where(row == 0, 0.0, pltpu.roll(value, 1, 0))
    part_ref[:, :, :, cells : cells + 8, :] = jnp.zeros((4, 6, 2, 8, width), jnp.float32)
    mine, other = 5 * core, 5 * (1 - core)

    for which in range(2):
        for f in range(3):
            for block in range(2):
                if which == 0:
                    plane_ref[mine, f, block] = give_ref[6 + f, block]
                    plane_ref[other, f, block] = take_ref[6 + f, block]
                    for x in range(4):
                        plane_ref[1 + x, f, block] = node_ref[x, f, block, 8 : 8 + cells, :]
                else:
                    plane_ref[mine, f, block] = give_ref[f, block]
                    plane_ref[other, f, block] = take_ref[f, block]
                    plane_ref[1 + 3 * core, f, block] = give_ref[3 + f, block]
                    plane_ref[4 - 3 * core, f, block] = take_ref[3 + f, block]
                    for x in range(2):
                        plane_ref[2 + x, f, block] = image_ref[x, f, block]
        if which == 0:
            for block in range(2):
                outer_elem_ref[block] = jnp.where(core == 0, take_ref[9, block], give_ref[9, block])

        @pl.loop(0, 6)
        def _(x):
            for field in range(3):
                def read(block, start, size):
                    value = plane_ref[x, field, block]
                    return value if start == 8 else below(value)
                store_modes(mode_ref, x, field, 3, read, cells)

        @pl.loop(0, 2 * tiles)
        def _(t):
            block, rows = t // tiles, pl.ds(pl.multiple_of((t % tiles) * 8, 8), 8)
            load = lambda x: [[mode_ref[x, 3 * f + k, block, rows, :] for k in range(3)] for f in range(3)]
            low, kept = load(0), None
            for x in range(1, 6):
                high = load(x)
                by_z = [high[f][1] + low[f][1] for f in range(3)]
                by_x = [high[f][0] - low[f][0] for f in range(3)]
                by_y = [high[f][2] + low[f][2] for f in range(3)]
                scaled = (elem_ref[x - 1, block, rows, :] if x < 5 else outer_elem_ref[block, rows, :]) * (0.25 * SHEAR)
                trace = RATIO * (by_z[0] + by_x[1] + by_y[2])
                now = [
                    scaled * (trace + 2.0 * by_z[0]),
                    scaled * (trace + 2.0 * by_x[1]),
                    scaled * (trace + 2.0 * by_y[2]),
                    scaled * (by_x[0] + by_z[1]),
                    scaled * (by_y[1] + by_x[2]),
                    scaled * (by_y[0] + by_z[2]),
                ]
                if kept is not None:
                    for k in range(6):
                        part_ref[x - 2, k, block, rows, :] = kept[k] + now[k]
                low, kept = high, now

        for x in range(4):
            count = jnp.where(row == cells - 1, 1.0, 0.5) * (jnp.where(last, 1.0, 0.5) if x == 3 else 0.5)
            count = count * jnp.where((lane == width - 1) & (core == 1), 1.0, 0.5)
            for k in range(6):
                both = [part_ref[x, k, block, 0:cells, :] + part_ref[x, k, block, 1 : cells + 1, :] for block in range(2)]
                beside = from_right(*both)
                value = jnp.where(core == 0, both[0] + beside[0], both[1] + beside[1])
                basis_ref[6 * which + k, pl.ds(x, cells, stride=4), :] = value * count
    for x in range(4):
        for f in range(3):
            basis_ref[12 + f, pl.ds(x, cells, stride=4), :] = plane_ref[1 + x, f, core]


def combine_kernel(sums_ref, force_ref, basis_ref, field_ref, stress_ref):
    total = jnp.sum(jnp.sum(sums_ref[...], axis=0), axis=1, keepdims=True)
    norm, cross, square, energy = (total[k : k + 1, :] for k in range(4))
    first = norm / cross
    norm_next = norm - 2.0 * first * cross + first * first * square
    ratio = norm_next / norm
    grown = 1.0 + ratio
    curvature = grown * grown * cross - 2.0 * grown * first * square + first * first * energy
    second = norm_next / curvature
    weight = jnp.broadcast_to(first + second * grown, force_ref.shape[1:])
    weight_image = jnp.broadcast_to(-second * first, force_ref.shape[1:])
    for f in range(3):
        field_ref[f] = weight * force_ref[f] + weight_image * basis_ref[12 + f]
    for k in range(6):
        stress_ref[k] = weight * basis_ref[k] + weight_image * basis_ref[6 + k]


def cost(flops, size):
    return pl.CostEstimate(flops=flops, bytes_accessed=size, transcendentals=0)


def per_device(body_force, modulus):
    cells, planes, width = modulus.shape
    slabs, cores = lax.axis_size("gx"), lax.axis_size("gy")
    assert planes == 4 and cores == 2 and cells % 8 == 0
    both = ("gx", "gy")
    f32 = jnp.float32
    shape = lambda *dims: jax.ShapeDtypeStruct(dims, f32)
    scratch = lambda *dims: pltpu.VMEM(dims, f32)

    force, own, same, cross = pl.pallas_call(
        pack_kernel,
        out_shape=(shape(3, cells * 4, width), shape(4, 4, cells, width), shape(2, 4, cells, width), shape(2, 4, cells, width)),
        in_specs=[pl.BlockSpec(memory_space=pl.ANY)] * 2,
        out_specs=[VMEM] * 4,
        scratch_shapes=[scratch(cells * 4, width), pltpu.SemaphoreType.DMA((2,))],
        compiler_params=LIMIT,
        name="pack",
    )(
        pltpu.with_memory_space_constraint(body_force.reshape(3, cells * 4, width), pltpu.HBM),
        pltpu.with_memory_space_constraint(modulus.reshape(cells * 4, width), pltpu.HBM),
    )

    up = [(2 * g, 2 * g + 2) for g in range(slabs - 1)]
    down = [(2 * g + 3, 2 * g + 1) for g in range(slabs - 1)]
    pairs = [(2 * g + 1, 2 * g + 2) for g in range(slabs - 1)]
    mate = lax.ppermute(own, "gy", [(0, 1), (1, 0)])
    cross_in = lax.ppermute(cross, both, pairs + [(q, p) for p, q in pairs])
    same_in = lax.ppermute(same, both, up + down)

    node, elem, image, edge_mode, edge_part, part_sums = pl.pallas_call(
        inner_kernel,
        out_shape=(
            shape(4, 3, 2, 8 + cells, width),
            shape(4, 2, cells, width),
            shape(2, 3, 2, cells, width),
            shape(12, 2, cells, width),
            shape(12, 2, cells, width),
            shape(3, 8, width),
        ),
        in_specs=[VMEM] * 2,
        out_specs=[VMEM] * 6,
        scratch_shapes=[scratch(4, 12, 2, cells, width), scratch(2, 12, 2, 8 + cells, width)],
        compiler_params=LIMIT,
        cost_estimate=cost(20_000_000, 4_000_000),
        name="inner",
    )(own, mate)
    give, sums = pl.pallas_call(
        outer_kernel,
        out_shape=(shape(10, 2, cells, width), shape(slabs * cores, 8, width)),
        in_specs=[VMEM] * 8,
        out_specs=[VMEM] * 2,
        scratch_shapes=[
            scratch(2, 3, 2, 8 + cells, width),
            scratch(2, 2, cells, width),
            scratch(3, 12, 2, cells, width),
            scratch(2, 12, 2, 8 + cells, width),
            scratch(3, 12, 2, cells, width),
        ],
        compiler_params=LIMIT,
        cost_estimate=cost(10_000_000, 3_000_000),
        name="outer",
    )(node, elem, image, edge_mode, edge_part, part_sums, same_in, cross_in)

    take = lax.ppermute(give, "gy", [(0, 1), (1, 0)])
    sums = lax.all_to_all(sums, both, 0, 0)
    basis = pl.pallas_call(
        stress_kernel,
        out_shape=shape(15, cells * 4, width),
        in_specs=[VMEM] * 5,
        out_specs=VMEM,
        scratch_shapes=[
            scratch(6, 3, 2, cells, width),
            scratch(2, cells, width),
            scratch(6, 9, 2, cells, width),
            scratch(4, 6, 2, 8 + cells, width),
        ],
        compiler_params=LIMIT,
        cost_estimate=cost(20_000_000, 4_000_000),
        name="stress",
    )(node, elem, image, give, take)

    field, stress = pl.pallas_call(
        combine_kernel,
        out_shape=(shape(3, cells * 4, width), shape(6, cells * 4, width)),
        in_specs=[VMEM] * 3,
        out_specs=[VMEM] * 2,
        compiler_params=LIMIT,
        name="combine",
    )(sums, force, basis)
    return field.reshape(3, cells, 4, width), stress.reshape(6, cells, 4, width)


def solution(mesh):
    return jax.shard_map(
        per_device,
        mesh=mesh,
        in_specs=(P(None, "sample", "gx", "gy"), P("sample", "gx", "gy")),
        out_specs=(P(None, "sample", "gx", "gy"), P(None, "sample", "gx", "gy")),
        check_vma=False,
    )
```

```python
import functools

import jax
import jax.numpy as jnp
from jax import lax
from jax.experimental import pallas as pl
from jax.experimental.pallas import tpu as pltpu
from jax.sharding import PartitionSpec as P

POISSON = 0.3
LAME = POISSON / ((1.0 + POISSON) * (1.0 - 2.0 * POISSON))
SHEAR = 1.0 / (2.0 * (1.0 + POISSON))
RATIO = LAME / SHEAR
ONE = SHEAR / 16.0
TWO = SHEAR / 48.0
THREE = (LAME + 4.0 * SHEAR) / 144.0

VMEM = pl.BlockSpec(memory_space=pltpu.VMEM)
LIMIT = pltpu.CompilerParams(vmem_limit_bytes=48 << 20)


def lanes(shape):
    return lax.broadcasted_iota(jnp.int32, shape, len(shape) - 1)


def from_left(first, second):
    edge = lanes(first.shape) == 0
    turned, turned2 = pltpu.roll(first, 1, 1), pltpu.roll(second, 1, 1)
    return jnp.where(edge, 0.0, turned), jnp.where(edge, turned, turned2)


def from_right(first, second):
    edge = lanes(first.shape) == first.shape[1] - 1
    turned, turned2 = (pltpu.roll(v, v.shape[1] - 1, 1) for v in (first, second))
    return jnp.where(edge, turned2, turned), jnp.where(edge, 0.0, turned2)


def pack_kernel(force_hbm, modulus_hbm, force_ref, own_ref, same_ref, cross_ref, modulus_ref, sem):
    core = lax.axis_index("gy")
    cells = own_ref.shape[2]
    copies = [
        pltpu.make_async_copy(force_hbm, force_ref, sem.at[0]),
        pltpu.make_async_copy(modulus_hbm, modulus_ref, sem.at[1]),
    ]
    for copy in copies:
        copy.start()
    for copy in copies:
        copy.wait()

    def plane(field, x):
        rows = pl.ds(x, cells, stride=4)
        return force_ref[field, rows, :] if field < 3 else modulus_ref[rows, :]

    for field in range(4):
        for x in range(4):
            own_ref[x, field] = plane(field, x)
        for i in range(2):
            same_ref[i, field] = plane(field, 2 * (1 - core) + i)
            cross_ref[i, field] = plane(field, 2 * core + i)


def below(value):
    row = lax.broadcasted_iota(jnp.int32, value.shape, 0)
    return jnp.where(row == 0, 0.0, pltpu.roll(value, 1, 0))


def plane_modes(high, low):
    sums = [h + l for h, l in zip(high, low)]
    diffs = [h - l for h, l in zip(high, low)]
    sums_left, diffs_left = from_left(*sums), from_left(*diffs)
    out = []
    for block in range(2):
        s, d, sl, dl = sums[block], diffs[block], sums_left[block], diffs_left[block]
        out.append((s + sl, d + dl, s - sl, d - dl))
    return out


def store_modes(mode_ref, at, field, kinds, high, low=None):
    found = plane_modes(high, [below(value) for value in high] if low is None else low)
    for block in range(2):
        for kind in range(kinds):
            mode_ref[at, kinds * field + kind, block] = found[block][kind]


def element_modes(low, high):
    found = []
    for component in range(3):
        modes = {}
        for kind, (z, y) in enumerate(((0, 0), (1, 0), (0, 1), (1, 1))):
            lo, hi = low[component][kind], high[component][kind]
            if (z, y) != (0, 0):
                modes[z, 0, y] = hi + lo
            modes[z, 1, y] = hi - lo
        found.append(modes)
    return found


def mode_forces(modes, modulus):
    u, v, w = modes
    one, two, three = modulus * ONE, modulus * TWO, modulus * THREE
    trace = RATIO * (u[1, 0, 0] + v[0, 1, 0] + w[0, 0, 1])
    shear_zx = one * (u[0, 1, 0] + v[1, 0, 0])
    shear_xy = one * (v[0, 0, 1] + w[0, 1, 0])
    shear_zy = one * (u[0, 0, 1] + w[1, 0, 0])
    trace_z = RATIO * (v[1, 1, 0] + w[1, 0, 1])
    trace_x = RATIO * (u[1, 1, 0] + w[0, 1, 1])
    trace_y = RATIO * (u[1, 0, 1] + v[0, 1, 1])
    mixed_zx = u[0, 1, 1] + v[1, 0, 1]
    mixed_xy = v[1, 0, 1] + w[1, 1, 0]
    mixed_zy = u[0, 1, 1] + w[1, 1, 0]
    return (
        {
            (1, 0, 0): one * (trace + 2.0 * u[1, 0, 0]),
            (0, 1, 0): shear_zx,
            (0, 0, 1): shear_zy,
            (1, 1, 0): two * (trace_x + 3.0 * u[1, 1, 0]),
            (1, 0, 1): two * (trace_y + 3.0 * u[1, 0, 1]),
            (0, 1, 1): two * (mixed_zx + mixed_zy),
            (1, 1, 1): three * u[1, 1, 1],
        },
        {
            (0, 1, 0): one * (trace + 2.0 * v[0, 1, 0]),
            (1, 0, 0): shear_zx,
            (0, 0, 1): shear_xy,
            (1, 1, 0): two * (trace_z + 3.0 * v[1, 1, 0]),
            (0, 1, 1): two * (trace_y + 3.0 * v[0, 1, 1]),
            (1, 0, 1): two * (mixed_zx + mixed_xy),
            (1, 1, 1): three * v[1, 1, 1],
        },
        {
            (0, 0, 1): one * (trace + 2.0 * w[0, 0, 1]),
            (1, 0, 0): shear_zy,
            (0, 1, 0): shear_xy,
            (1, 0, 1): two * (trace_z + 3.0 * w[1, 0, 1]),
            (0, 1, 1): two * (trace_x + 3.0 * w[0, 1, 1]),
            (1, 1, 0): two * (mixed_xy + mixed_zy),
            (1, 1, 1): three * w[1, 1, 1],
        },
    )


def mode_energy(modes, modulus):
    u, v, w = modes
    square = lambda value: value * value
    a, b, c = u[1, 0, 0], v[0, 1, 0], w[0, 0, 1]
    one = RATIO * square(a + b + c) + 2.0 * (square(a) + square(b) + square(c))
    one = one + square(u[0, 1, 0] + v[1, 0, 0]) + square(v[0, 0, 1] + w[0, 1, 0]) + square(u[0, 0, 1] + w[1, 0, 0])
    d, e, f = u[1, 1, 0], u[1, 0, 1], v[1, 1, 0]
    g, h, k = v[0, 1, 1], w[1, 0, 1], w[0, 1, 1]
    two = RATIO * (square(f + h) + square(d + k) + square(e + g))
    two = two + 3.0 * (square(d) + square(e) + square(f) + square(g) + square(h) + square(k))
    m, n, o = u[0, 1, 1], v[1, 0, 1], w[1, 1, 0]
    two = two + square(m + n) + square(n + o) + square(m + o)
    three = square(u[1, 1, 1]) + square(v[1, 1, 1]) + square(w[1, 1, 1])
    return modulus * (ONE * one + TWO * two + THREE * three)


def face_forces(forces):
    upper, lower = [], []
    for component in range(3):
        up, down = [], []
        for z, y in ((0, 0), (1, 0), (0, 1), (1, 1)):
            diff, both = forces[component][z, 1, y], forces[component].get((z, 0, y))
            up.append(diff if both is None else both + diff)
            down.append(-diff if both is None else both - diff)
        upper.append(up)
        lower.append(down)
    return upper, lower


def corner_forces(modes):
    ss, ds, sd, dd = modes
    here, back = ss + ds, ss - ds
    here_y, back_y = sd + dd, sd - dd
    return here + here_y, here - here_y, back + back_y, back - back_y


def plus(first, second):
    return [[p + q for p, q in zip(a, b)] for a, b in zip(first, second)]


def assembled(part_ref, at, field, cells):
    here = lambda k, block: part_ref[at, 4 * field + k, block, 0:cells, :]
    above = lambda k, block: part_ref[at, 4 * field + k, block, 1 : cells + 1, :]
    beside = from_right(*(here(1, block) + above(3, block) for block in range(2)))
    return [here(0, block) + above(2, block) + beside[block] for block in range(2)]


def inner_kernel(own_ref, mate_ref, node_ref, elem_ref, image_ref, edge_part_ref, sums_ref, outer_mode_ref, image_mode_ref, mode_ref, part_ref):
    core = lax.axis_index("gy")
    cells, width = own_ref.shape[2:]
    tiles = cells // 8
    zeros = lambda *dims: jnp.zeros(dims, jnp.float32)
    node_ref[:, :, :, 0:8, :] = zeros(4, 3, 2, 8, width)
    for x in range(4):
        for ref, block in ((own_ref, core), (mate_ref, 1 - core)):
            for field in range(3):
                node_ref[x, field, block, 8 : 8 + cells, :] = ref[x, field]
            elem_ref[x, block] = ref[x, 3]

    @pl.loop(0, 4)
    def _(x):
        for field in range(3):
            high, low = ([node_ref[x, field, block, at : at + cells, :] for block in range(2)] for at in (8, 7))
            store_modes(mode_ref, x, field, 4, high, low)

    outer_mode_ref[2 * (1 - core)] = mode_ref[3 * core]
    part_ref[:, :, :, cells : cells + 8, :] = zeros(2, 12, 2, 8, width)

    @pl.loop(0, 2 * tiles, unroll=True)
    def _(t):
        block, rows = t // tiles, pl.ds(pl.multiple_of((t % tiles) * 8, 8), 8)
        load = lambda x: [[mode_ref[x, 4 * f + k, block, rows, :] for k in range(4)] for f in range(3)]
        low, kept, outer = load(0), None, None
        for x in range(1, 4):
            high = load(x)
            upper, lower = face_forces(mode_forces(element_modes(low, high), elem_ref[x, block, rows, :]))
            if kept is None:
                outer = lower
            else:
                for f, modes in enumerate(plus(kept, lower)):
                    for k, value in enumerate(corner_forces(modes)):
                        part_ref[x - 2, 4 * f + k, block, rows, :] = value
            low, kept = high, upper
        for f in range(3):
            for k in range(4):
                edge_part_ref[4 * f + k, block, rows, :] = jnp.where(core == 0, outer[f][k], kept[f][k])

    fold = lambda value: value.reshape(tiles, 8, width).sum(0)
    norm = cross = square = zeros(8, width)
    for i in range(2):
        mine = jnp.where(core == i, 1.0, 0.0)
        for f in range(3):
            values = assembled(part_ref, i, f, cells)
            store_modes(image_mode_ref, jnp.where(core == 0, 2 + i, i), f, 4, values)
            for block, value in enumerate(values):
                image_ref[i, f, block] = value
                force = node_ref[i + 1, f, block, 8 : 8 + cells, :]
                norm = norm + mine * fold(force * force)
                cross = cross + mine * fold(force * value)
                square = square + mine * fold(value * value)
    for k, value in enumerate((norm, cross, square)):
        sums_ref[k] = value


def outer_kernel(
    node_ref, elem_ref, edge_part_ref, part_sums_ref, same_ref, cross_ref, _outer_mode, _image_mode,
    give_ref, sums_ref, mode_ref, image_mode_ref, part_ref, halo_elem_ref,
):
    core, slab = lax.axis_index("gy"), lax.axis_index("gx")
    cells, width = same_ref.shape[2:]
    tiles = cells // 8
    zeros = lambda *dims: jnp.zeros(dims, jnp.float32)
    near = 1 - core
    first_core = core == 0
    for i in range(2):
        for f in range(4):
            same, cross = same_ref[i, f], cross_ref[i, f]
            values = [jnp.where(first_core, same, cross), jnp.where(first_core, cross, same)]
            if f < 3:
                store_modes(mode_ref, core + i, f, 4, values)
            else:
                halo_elem_ref[i, 0], halo_elem_ref[i, 1] = values
    for f in range(4):
        give_ref[6 + f, core] = same_ref[near, f]
        give_ref[6 + f, near] = cross_ref[near, f]

    part_ref[:, :, :, cells : cells + 8, :] = zeros(2, 12, 2, 8, width)

    @pl.loop(0, 2 * tiles, unroll=True)
    def _(t):
        block, rows = t // tiles, pl.ds(pl.multiple_of((t % tiles) * 8, 8), 8)
        load = lambda x: [[mode_ref[x, 4 * f + k, block, rows, :] for k in range(4)] for f in range(3)]
        planes = [load(x) for x in range(3)]
        first = halo_elem_ref[near, block, rows, :]
        second = jnp.where(first_core, elem_ref[0, block, rows, :], halo_elem_ref[1, block, rows, :])
        upper, lower = face_forces(mode_forces(element_modes(planes[0], planes[1]), first))
        upper2, lower2 = face_forces(mode_forces(element_modes(planes[1], planes[2]), second))
        for f, modes in enumerate(plus(upper, lower2)):
            for k, value in enumerate(corner_forces(modes)):
                part_ref[0, 4 * f + k, block, rows, :] = value
        for f in range(3):
            modes = [edge_part_ref[4 * f + k, block, rows, :] + jnp.where(first_core, upper2[f][k], lower[f][k]) for k in range(4)]
            for k, value in enumerate(corner_forces(modes)):
                part_ref[1, 4 * f + k, block, rows, :] = value

    clamped = jnp.where(first_core & (slab == 0), 0.0, 1.0)
    fold = lambda value: value.reshape(tiles, 8, width).sum(0)
    norm, cross, square = (part_sums_ref[k] for k in range(3))
    for f in range(3):
        values = [value * clamped for value in assembled(part_ref, 0, f, cells)]
        store_modes(image_mode_ref, 3 * core, f, 4, values)
        for block in range(2):
            give_ref[f, block] = values[block]
        values = assembled(part_ref, 1, f, cells)
        store_modes(image_mode_ref, 1 + core, f, 4, values)
        for block, value in enumerate(values):
            give_ref[3 + f, block] = value
            force = node_ref[3 * core, f, block, 8 : 8 + cells, :]
            norm = norm + fold(force * force)
            cross = cross + fold(force * value)
            square = square + fold(value * value)

    def energy_of(t, total):
        block, rows = t // tiles, pl.ds(pl.multiple_of((t % tiles) * 8, 8), 8)
        load = lambda x: [[image_mode_ref[x, 4 * f + k, block, rows, :] for k in range(4)] for f in range(3)]
        low = load(0)
        for x in range(2):
            high = load(x + 1)
            total = total + mode_energy(element_modes(low, high), elem_ref[2 * core + x, block, rows, :])
            low = high
        return total

    energy = lax.fori_loop(0, 2 * tiles, energy_of, zeros(8, width), unroll=True)
    line = lax.broadcasted_iota(jnp.int32, (8, width), 0)
    packed = zeros(8, width)
    for k, value in enumerate((norm, cross, square, energy)):
        packed = jnp.where(line == k, jnp.sum(value, axis=0, keepdims=True), packed)
    sums_ref[...] = jnp.broadcast_to(packed[None], sums_ref.shape)


def stress_kernel(
    node_ref, elem_ref, image_ref, give_ref, take_ref, basis_ref, plane_ref, outer_elem_ref, mode_ref, part_ref,
):
    core, slab = lax.axis_index("gy"), lax.axis_index("gx")
    last = slab == lax.axis_size("gx") - 1
    cells, width = elem_ref.shape[2:]
    tiles = cells // 8
    row = lax.broadcasted_iota(jnp.int32, (cells, width), 0)
    lane = lanes((cells, width))
    part_ref[:, :, :, cells : cells + 8, :] = jnp.zeros((4, 6, 2, 8, width), jnp.float32)
    mine, other = 5 * core, 5 * (1 - core)

    for which in range(2):
        for f in range(3):
            for block in range(2):
                if which == 0:
                    plane_ref[mine, f, block] = give_ref[6 + f, block]
                    plane_ref[other, f, block] = take_ref[6 + f, block]
                    for x in range(4):
                        plane_ref[1 + x, f, block] = node_ref[x, f, block, 8 : 8 + cells, :]
                else:
                    plane_ref[mine, f, block] = give_ref[f, block]
                    plane_ref[other, f, block] = take_ref[f, block]
                    plane_ref[1 + 3 * core, f, block] = give_ref[3 + f, block]
                    plane_ref[4 - 3 * core, f, block] = take_ref[3 + f, block]
                    for x in range(2):
                        plane_ref[2 + x, f, block] = image_ref[x, f, block]
        if which == 0:
            for block in range(2):
                outer_elem_ref[block] = jnp.where(core == 0, take_ref[9, block], give_ref[9, block])

        @pl.loop(0, 6)
        def _(x):
            for field in range(3):
                store_modes(mode_ref, x, field, 3, [plane_ref[x, field, block] for block in range(2)])

        @pl.loop(0, 2 * tiles, unroll=True)
        def _(t):
            block, rows = t // tiles, pl.ds(pl.multiple_of((t % tiles) * 8, 8), 8)
            load = lambda x: [[mode_ref[x, 3 * f + k, block, rows, :] for k in range(3)] for f in range(3)]
            low, kept = load(0), None
            for x in range(1, 6):
                high = load(x)
                by_z = [high[f][1] + low[f][1] for f in range(3)]
                by_x = [high[f][0] - low[f][0] for f in range(3)]
                by_y = [high[f][2] + low[f][2] for f in range(3)]
                scaled = (elem_ref[x - 1, block, rows, :] if x < 5 else outer_elem_ref[block, rows, :]) * (0.25 * SHEAR)
                trace = RATIO * (by_z[0] + by_x[1] + by_y[2])
                now = [
                    scaled * (trace + 2.0 * by_z[0]),
                    scaled * (trace + 2.0 * by_x[1]),
                    scaled * (trace + 2.0 * by_y[2]),
                    scaled * (by_x[0] + by_z[1]),
                    scaled * (by_y[1] + by_x[2]),
                    scaled * (by_y[0] + by_z[2]),
                ]
                if kept is not None:
                    for k in range(6):
                        part_ref[x - 2, k, block, rows, :] = kept[k] + now[k]
                low, kept = high, now

        for x in range(4):
            count = jnp.where(row == cells - 1, 1.0, 0.5) * (jnp.where(last, 1.0, 0.5) if x == 3 else 0.5)
            count = count * jnp.where((lane == width - 1) & (core == 1), 1.0, 0.5)
            for k in range(6):
                both = [part_ref[x, k, block, 0:cells, :] + part_ref[x, k, block, 1 : cells + 1, :] for block in range(2)]
                beside = from_right(*both)
                value = jnp.where(core == 0, both[0] + beside[0], both[1] + beside[1])
                basis_ref[6 * which + k, pl.ds(x, cells, stride=4), :] = value * count
    for x in range(4):
        for f in range(3):
            basis_ref[12 + f, pl.ds(x, cells, stride=4), :] = plane_ref[1 + x, f, core]


def combine_kernel(sums_ref, force_ref, basis_ref, field_ref, stress_ref):
    total = jnp.sum(jnp.sum(sums_ref[...], axis=0), axis=1, keepdims=True)
    norm, cross, square, energy = (total[k : k + 1, :] for k in range(4))
    first = norm / cross
    norm_next = norm - 2.0 * first * cross + first * first * square
    ratio = norm_next / norm
    grown = 1.0 + ratio
    curvature = grown * grown * cross - 2.0 * grown * first * square + first * first * energy
    second = norm_next / curvature
    weight = jnp.broadcast_to(first + second * grown, force_ref.shape[1:])
    weight_image = jnp.broadcast_to(-second * first, force_ref.shape[1:])
    for f in range(3):
        field_ref[f] = weight * force_ref[f] + weight_image * basis_ref[12 + f]
    for k in range(6):
        stress_ref[k] = weight * basis_ref[k] + weight_image * basis_ref[6 + k]


def cost(flops, size):
    return pl.CostEstimate(flops=flops, bytes_accessed=size, transcendentals=0)


def per_device(body_force, modulus):
    cells, planes, width = modulus.shape
    slabs, cores = lax.axis_size("gx"), lax.axis_size("gy")
    assert planes == 4 and cores == 2 and cells % 8 == 0
    both = ("gx", "gy")
    f32 = jnp.float32
    shape = lambda *dims: jax.ShapeDtypeStruct(dims, f32)
    scratch = lambda *dims: pltpu.VMEM(dims, f32)

    force, own, same, cross = pl.pallas_call(
        pack_kernel,
        out_shape=(shape(3, cells * 4, width), shape(4, 4, cells, width), shape(2, 4, cells, width), shape(2, 4, cells, width)),
        in_specs=[pl.BlockSpec(memory_space=pl.ANY)] * 2,
        out_specs=[VMEM] * 4,
        scratch_shapes=[scratch(cells * 4, width), pltpu.SemaphoreType.DMA((2,))],
        compiler_params=LIMIT,
        name="pack",
    )(
        pltpu.with_memory_space_constraint(body_force.reshape(3, cells * 4, width), pltpu.HBM),
        pltpu.with_memory_space_constraint(modulus.reshape(cells * 4, width), pltpu.HBM),
    )

    up = [(2 * g, 2 * g + 2) for g in range(slabs - 1)]
    down = [(2 * g + 3, 2 * g + 1) for g in range(slabs - 1)]
    pairs = [(2 * g + 1, 2 * g + 2) for g in range(slabs - 1)]
    mate = lax.ppermute(own, "gy", [(0, 1), (1, 0)])
    cross_in = lax.ppermute(cross, both, pairs + [(q, p) for p, q in pairs])
    same_in = lax.ppermute(same, both, up + down)

    modes = lambda planes: shape(planes, 12, 2, cells, width)
    node, elem, image, edge_part, part_sums, outer_mode, image_mode = pl.pallas_call(
        inner_kernel,
        out_shape=(
            shape(4, 3, 2, 8 + cells, width),
            shape(4, 2, cells, width),
            shape(2, 3, 2, cells, width),
            shape(12, 2, cells, width),
            shape(3, 8, width),
            modes(3),
            modes(4),
        ),
        in_specs=[VMEM] * 2,
        out_specs=[VMEM] * 7,
        scratch_shapes=[scratch(4, 12, 2, cells, width), scratch(2, 12, 2, 8 + cells, width)],
        compiler_params=LIMIT,
        cost_estimate=cost(20_000_000, 4_000_000),
        name="inner",
    )(own, mate)
    give, sums, _, _ = pl.pallas_call(
        outer_kernel,
        out_shape=(shape(10, 2, cells, width), shape(slabs * cores, 8, width), modes(3), modes(4)),
        in_specs=[VMEM] * 8,
        out_specs=[VMEM] * 4,
        input_output_aliases={6: 2, 7: 3},
        scratch_shapes=[scratch(2, 12, 2, 8 + cells, width), scratch(2, 2, cells, width)],
        compiler_params=LIMIT,
        cost_estimate=cost(10_000_000, 3_000_000),
        name="outer",
    )(node, elem, edge_part, part_sums, same_in, cross_in, outer_mode, image_mode)

    take = lax.ppermute(give, "gy", [(0, 1), (1, 0)])
    sums = lax.all_to_all(sums, both, 0, 0, axis_index_groups=[list(range(slabs * cores))[::-1]])
    basis = pl.pallas_call(
        stress_kernel,
        out_shape=shape(15, cells * 4, width),
        in_specs=[VMEM] * 5,
        out_specs=VMEM,
        scratch_shapes=[
            scratch(6, 3, 2, cells, width),
            scratch(2, cells, width),
            scratch(6, 9, 2, cells, width),
            scratch(4, 6, 2, 8 + cells, width),
        ],
        compiler_params=LIMIT,
        cost_estimate=cost(20_000_000, 4_000_000),
        name="stress",
    )(node, elem, image, give, take)

    field, stress = pl.pallas_call(
        combine_kernel,
        out_shape=(shape(3, cells * 4, width), shape(6, cells * 4, width)),
        in_specs=[VMEM] * 3,
        out_specs=[VMEM] * 2,
        compiler_params=LIMIT,
        name="combine",
    )(sums, force, basis)
    return field.reshape(3, cells, 4, width), stress.reshape(6, cells, 4, width)


def solution(mesh):
    return jax.shard_map(
        per_device,
        mesh=mesh,
        in_specs=(P(None, "sample", "gx", "gy"), P("sample", "gx", "gy")),
        out_specs=(P(None, "sample", "gx", "gy"), P(None, "sample", "gx", "gy")),
        check_vma=False,
    )
```

```python
import functools

import jax
import jax.numpy as jnp
from jax import lax
from jax.experimental import pallas as pl
from jax.experimental.pallas import tpu as pltpu
from jax.sharding import PartitionSpec as P

POISSON = 0.3
LAME = POISSON / ((1.0 + POISSON) * (1.0 - 2.0 * POISSON))
SHEAR = 1.0 / (2.0 * (1.0 + POISSON))
RATIO = LAME / SHEAR
ONE = SHEAR / 16.0
TWO = SHEAR / 48.0
THREE = (LAME + 4.0 * SHEAR) / 144.0

VMEM = pl.BlockSpec(memory_space=pltpu.VMEM)
LIMIT = pltpu.CompilerParams(vmem_limit_bytes=48 << 20)


def lanes(shape):
    return lax.broadcasted_iota(jnp.int32, shape, len(shape) - 1)


def from_left(first, second):
    edge = lanes(first.shape) == 0
    turned, turned2 = pltpu.roll(first, 1, 1), pltpu.roll(second, 1, 1)
    return jnp.where(edge, 0.0, turned), jnp.where(edge, turned, turned2)


def from_right(first, second):
    edge = lanes(first.shape) == first.shape[1] - 1
    turned, turned2 = (pltpu.roll(v, v.shape[1] - 1, 1) for v in (first, second))
    return jnp.where(edge, turned2, turned), jnp.where(edge, 0.0, turned2)


def pack_kernel(force_hbm, modulus_hbm, own_ref, same_ref, cross_ref, force_ref, modulus_ref, sem):
    core = lax.axis_index("gy")
    cells = own_ref.shape[2]
    copies = [
        pltpu.make_async_copy(force_hbm, force_ref, sem.at[0]),
        pltpu.make_async_copy(modulus_hbm, modulus_ref, sem.at[1]),
    ]
    for copy in copies:
        copy.start()
    for copy in copies:
        copy.wait()

    def plane(field, x):
        rows = pl.ds(x, cells, stride=4)
        return force_ref[field, rows, :] if field < 3 else modulus_ref[rows, :]

    for field in range(4):
        for x in range(4):
            own_ref[x, field] = plane(field, x)
        for i in range(2):
            same_ref[i, field] = plane(field, 2 * (1 - core) + i)
            cross_ref[i, field] = plane(field, 2 * core + i)


def below(value):
    row = lax.broadcasted_iota(jnp.int32, value.shape, 0)
    return jnp.where(row == 0, 0.0, pltpu.roll(value, 1, 0))


def store_modes(mode_ref, at, field, high, low=None, last_ref=None):
    base = 4 * field if last_ref is None else 3 * field
    left = from_left(*high)
    for block in range(2):
        value, beside = high[block], left[block]
        value_low = below(value) if low is None else low[block]
        beside_low = below(beside)
        total, total_beside = value + value_low, beside + beside_low
        slope, slope_beside = value - value_low, beside - beside_low
        mode_ref[at, base, block] = total + total_beside
        mode_ref[at, base + 1, block] = slope + slope_beside
        mode_ref[at, base + 2, block] = total - total_beside
        if last_ref is None:
            mode_ref[at, base + 3, block] = slope - slope_beside
        else:
            last_ref[at, field, block] = slope - slope_beside


def element_modes(low, high):
    found = []
    for component in range(3):
        modes = {}
        for kind, (z, y) in enumerate(((0, 0), (1, 0), (0, 1), (1, 1))):
            lo, hi = low[component][kind], high[component][kind]
            if (z, y) != (0, 0):
                modes[z, 0, y] = hi + lo
            modes[z, 1, y] = hi - lo
        found.append(modes)
    return found


def mode_forces(modes, modulus):
    u, v, w = modes
    one, two, three = modulus * ONE, modulus * TWO, modulus * THREE
    trace = RATIO * (u[1, 0, 0] + v[0, 1, 0] + w[0, 0, 1])
    shear_zx = one * (u[0, 1, 0] + v[1, 0, 0])
    shear_xy = one * (v[0, 0, 1] + w[0, 1, 0])
    shear_zy = one * (u[0, 0, 1] + w[1, 0, 0])
    trace_z = RATIO * (v[1, 1, 0] + w[1, 0, 1])
    trace_x = RATIO * (u[1, 1, 0] + w[0, 1, 1])
    trace_y = RATIO * (u[1, 0, 1] + v[0, 1, 1])
    mixed_zx = u[0, 1, 1] + v[1, 0, 1]
    mixed_xy = v[1, 0, 1] + w[1, 1, 0]
    mixed_zy = u[0, 1, 1] + w[1, 1, 0]
    return (
        {
            (1, 0, 0): one * (trace + 2.0 * u[1, 0, 0]),
            (0, 1, 0): shear_zx,
            (0, 0, 1): shear_zy,
            (1, 1, 0): two * (trace_x + 3.0 * u[1, 1, 0]),
            (1, 0, 1): two * (trace_y + 3.0 * u[1, 0, 1]),
            (0, 1, 1): two * (mixed_zx + mixed_zy),
            (1, 1, 1): three * u[1, 1, 1],
        },
        {
            (0, 1, 0): one * (trace + 2.0 * v[0, 1, 0]),
            (1, 0, 0): shear_zx,
            (0, 0, 1): shear_xy,
            (1, 1, 0): two * (trace_z + 3.0 * v[1, 1, 0]),
            (0, 1, 1): two * (trace_y + 3.0 * v[0, 1, 1]),
            (1, 0, 1): two * (mixed_zx + mixed_xy),
            (1, 1, 1): three * v[1, 1, 1],
        },
        {
            (0, 0, 1): one * (trace + 2.0 * w[0, 0, 1]),
            (1, 0, 0): shear_zy,
            (0, 1, 0): shear_xy,
            (1, 0, 1): two * (trace_z + 3.0 * w[1, 0, 1]),
            (0, 1, 1): two * (trace_x + 3.0 * w[0, 1, 1]),
            (1, 1, 0): two * (mixed_xy + mixed_zy),
            (1, 1, 1): three * w[1, 1, 1],
        },
    )


def mode_energy(modes, modulus):
    u, v, w = modes
    square = lambda value: value * value
    a, b, c = u[1, 0, 0], v[0, 1, 0], w[0, 0, 1]
    one = RATIO * square(a + b + c) + 2.0 * (square(a) + square(b) + square(c))
    one = one + square(u[0, 1, 0] + v[1, 0, 0]) + square(v[0, 0, 1] + w[0, 1, 0]) + square(u[0, 0, 1] + w[1, 0, 0])
    d, e, f = u[1, 1, 0], u[1, 0, 1], v[1, 1, 0]
    g, h, k = v[0, 1, 1], w[1, 0, 1], w[0, 1, 1]
    two = RATIO * (square(f + h) + square(d + k) + square(e + g))
    two = two + 3.0 * (square(d) + square(e) + square(f) + square(g) + square(h) + square(k))
    m, n, o = u[0, 1, 1], v[1, 0, 1], w[1, 1, 0]
    two = two + square(m + n) + square(n + o) + square(m + o)
    three = square(u[1, 1, 1]) + square(v[1, 1, 1]) + square(w[1, 1, 1])
    return modulus * (ONE * one + TWO * two + THREE * three)


def face_forces(forces):
    upper, lower = [], []
    for component in range(3):
        up, down = [], []
        for z, y in ((0, 0), (1, 0), (0, 1), (1, 1)):
            diff, both = forces[component][z, 1, y], forces[component].get((z, 0, y))
            up.append(diff if both is None else both + diff)
            down.append(-diff if both is None else both - diff)
        upper.append(up)
        lower.append(down)
    return upper, lower


def corner_forces(modes):
    ss, ds, sd, dd = modes
    here, back = ss + ds, ss - ds
    here_y, back_y = sd + dd, sd - dd
    return here + here_y, here - here_y, back + back_y, back - back_y


def plus(first, second):
    return [[p + q for p, q in zip(a, b)] for a, b in zip(first, second)]


def pick(flag, first, second):
    return [[jnp.where(flag, p, q) for p, q in zip(a, b)] for a, b in zip(first, second)]


def assembled(part_ref, at, field, cells):
    here = lambda k, block: part_ref[at, 4 * field + k, block, 0:cells, :]
    above = lambda k, block: part_ref[at, 4 * field + k, block, 1 : cells + 1, :]
    beside = from_right(*(here(1, block) + above(3, block) for block in range(2)))
    return [here(0, block) + above(2, block) + beside[block] for block in range(2)]


def mode_stress(low, high, modulus):
    by_z = [high[f][1] + low[f][1] for f in range(3)]
    by_x = [high[f][0] - low[f][0] for f in range(3)]
    by_y = [high[f][2] + low[f][2] for f in range(3)]
    scaled = modulus * (0.25 * SHEAR)
    trace = RATIO * (by_z[0] + by_x[1] + by_y[2])
    return [
        scaled * (trace + 2.0 * by_z[0]),
        scaled * (trace + 2.0 * by_x[1]),
        scaled * (trace + 2.0 * by_y[2]),
        scaled * (by_x[0] + by_z[1]),
        scaled * (by_y[1] + by_x[2]),
        scaled * (by_y[0] + by_z[2]),
    ]


def nodal_average(part_ref, at, k, core, count_x):
    cells, width = part_ref.shape[3] - 8, part_ref.shape[4]
    both = [part_ref[at, k, block, 0:cells, :] + part_ref[at, k, block, 1 : cells + 1, :] for block in range(2)]
    first, second = both
    lane = lanes((cells, width))
    row = lax.broadcasted_iota(jnp.int32, (cells, width), 0)
    mine = jnp.where(core == 0, first, second)
    turned = pltpu.roll(jnp.where(lane == 0, jnp.where(core == 0, second, 0.0), mine), width - 1, 1)
    count = jnp.where(row == cells - 1, 1.0, 0.5) * jnp.where((lane == width - 1) & (core == 1), 1.0, 0.5)
    return (mine + turned) * (count * count_x)


def inner_kernel(
    own_ref, mate_ref, ends_ref, elem_ref, edge_part_ref, sums_ref, edge_mode_ref, image_mode_ref, image_last_ref, side_ref, early_ref,
    node_ref, mode_ref, part_ref, stress_part_ref,
):
    core = lax.axis_index("gy")
    cells, width = own_ref.shape[2:]
    tiles = cells // 8
    zeros = lambda *dims: jnp.zeros(dims, jnp.float32)
    node_ref[:, :, :, 0:8, :] = zeros(4, 3, 2, 8, width)
    for x in range(4):
        for ref, block in ((own_ref, core), (mate_ref, 1 - core)):
            for field in range(3):
                node_ref[x, field, block, 8 : 8 + cells, :] = ref[x, field]
                if x in (0, 3):
                    ends_ref[x // 3, field, block] = ref[x, field]
            elem_ref[x, block] = ref[x, 3]

    @pl.loop(0, 4)
    def _(x):
        for field in range(3):
            high, low = ([node_ref[x, field, block, at : at + cells, :] for block in range(2)] for at in (8, 7))
            store_modes(mode_ref, x, field, high, low)

    edge_mode_ref[...] = mode_ref[3 * core]
    part_ref[:, :, :, cells : cells + 8, :] = zeros(2, 12, 2, 8, width)
    stress_part_ref[:, :, :, cells : cells + 8, :] = zeros(2, 6, 2, 8, width)

    @pl.loop(0, 2 * tiles, unroll=True)
    def _(t):
        block, rows = t // tiles, pl.ds(pl.multiple_of((t % tiles) * 8, 8), 8)
        load = lambda x: [[mode_ref[x, 4 * f + k, block, rows, :] for k in range(4)] for f in range(3)]
        low, kept, outer = load(0), None, None
        for x in range(1, 4):
            high = load(x)
            upper, lower = face_forces(mode_forces(element_modes(low, high), elem_ref[x, block, rows, :]))
            if kept is None:
                outer = lower
            else:
                for f, modes in enumerate(plus(kept, lower)):
                    for k, value in enumerate(corner_forces(modes)):
                        part_ref[x - 2, 4 * f + k, block, rows, :] = value
            low, kept = high, upper
        for f in range(3):
            for k in range(4):
                edge_part_ref[4 * f + k, block, rows, :] = jnp.where(core == 0, outer[f][k], kept[f][k])

    @pl.loop(0, 2 * tiles, unroll=True)
    def _(t):
        block, rows = t // tiles, pl.ds(pl.multiple_of((t % tiles) * 8, 8), 8)
        load = lambda x: [[mode_ref[x, 4 * f + k, block, rows, :] for k in range(3)] for f in range(3)]
        low, kept = load(0), None
        for x in range(1, 4):
            high = load(x)
            now = mode_stress(low, high, elem_ref[x, block, rows, :])
            for k in range(6):
                if x > 1:
                    stress_part_ref[x - 2, k, block, rows, :] = kept[k] + now[k]
                if x != 2:
                    side_ref[x // 2, k, block, rows, :] = now[k]
            low, kept = high, now

    fold = lambda value: value.reshape(tiles, 8, width).sum(0)
    norm = cross = square = zeros(8, width)
    for i in range(2):
        mine = jnp.where(core == i, 1.0, 0.0)
        for f in range(3):
            values = assembled(part_ref, i, f, cells)
            store_modes(image_mode_ref, i, f, values, last_ref=image_last_ref)
            early_ref[i, 6 + f] = jnp.where(core == 0, values[0], values[1])
            early_ref[i, 9 + f] = own_ref[1 + i, f]
            for block, value in enumerate(values):
                force = node_ref[i + 1, f, block, 8 : 8 + cells, :]
                norm = norm + mine * fold(force * force)
                cross = cross + mine * fold(force * value)
                square = square + mine * fold(value * value)
        for k in range(6):
            early_ref[i, k] = nodal_average(stress_part_ref, i, k, core, 0.5)
    for k, value in enumerate((norm, cross, square)):
        sums_ref[k] = value


def outer_kernel(
    ends_ref, elem_ref, edge_part_ref, part_sums_ref, edge_mode_ref, image_mode_ref, image_last_ref, same_ref, cross_ref,
    give_ref, sums_ref, halo_mode_ref, face_mode_ref, part_ref, halo_elem_ref,
):
    core, slab = lax.axis_index("gy"), lax.axis_index("gx")
    cells, width = same_ref.shape[2:]
    tiles = cells // 8
    zeros = lambda *dims: jnp.zeros(dims, jnp.float32)
    near = 1 - core
    first_core = core == 0
    for i in range(2):
        for f in range(4):
            same, cross = same_ref[i, f], cross_ref[i, f]
            values = [jnp.where(first_core, same, cross), jnp.where(first_core, cross, same)]
            if f < 3:
                store_modes(halo_mode_ref, i, f, values)
            else:
                halo_elem_ref[i, 0], halo_elem_ref[i, 1] = values
    for f in range(4):
        give_ref[6 + f, core] = same_ref[near, f]
        give_ref[6 + f, near] = cross_ref[near, f]

    part_ref[:, :, :, cells : cells + 8, :] = zeros(2, 12, 2, 8, width)

    @pl.loop(0, 2 * tiles, unroll=True)
    def _(t):
        block, rows = t // tiles, pl.ds(pl.multiple_of((t % tiles) * 8, 8), 8)
        load = lambda at: [[halo_mode_ref[at, 4 * f + k, block, rows, :] for k in range(4)] for f in range(3)]
        edge = [[edge_mode_ref[4 * f + k, block, rows, :] for k in range(4)] for f in range(3)]
        halo = [load(0), load(1)]
        planes = [pick(first_core, halo[0], edge), pick(first_core, halo[1], halo[0]), pick(first_core, edge, halo[1])]
        first = halo_elem_ref[near, block, rows, :]
        second = jnp.where(first_core, elem_ref[0, block, rows, :], halo_elem_ref[1, block, rows, :])
        upper, lower = face_forces(mode_forces(element_modes(planes[0], planes[1]), first))
        upper2, lower2 = face_forces(mode_forces(element_modes(planes[1], planes[2]), second))
        for f, modes in enumerate(plus(upper, lower2)):
            for k, value in enumerate(corner_forces(modes)):
                part_ref[0, 4 * f + k, block, rows, :] = value
        for f in range(3):
            modes = [edge_part_ref[4 * f + k, block, rows, :] + jnp.where(first_core, upper2[f][k], lower[f][k]) for k in range(4)]
            for k, value in enumerate(corner_forces(modes)):
                part_ref[1, 4 * f + k, block, rows, :] = value

    clamped = jnp.where(first_core & (slab == 0), 0.0, 1.0)
    fold = lambda value: value.reshape(tiles, 8, width).sum(0)
    norm, cross, square = (part_sums_ref[k] for k in range(3))
    for f in range(3):
        values = [value * clamped for value in assembled(part_ref, 0, f, cells)]
        store_modes(face_mode_ref, 0, f, values)
        for block in range(2):
            give_ref[f, block] = values[block]
        values = assembled(part_ref, 1, f, cells)
        store_modes(face_mode_ref, 1, f, values)
        for block, value in enumerate(values):
            give_ref[3 + f, block] = value
            force = ends_ref[core, f, block]
            norm = norm + fold(force * force)
            cross = cross + fold(force * value)
            square = square + fold(value * value)

    def energy_of(t, total):
        block, rows = t // tiles, pl.ds(pl.multiple_of((t % tiles) * 8, 8), 8)
        load = lambda ref, at: [[ref[at, 4 * f + k, block, rows, :] for k in range(4)] for f in range(3)]
        inner, beyond = (
            [[image_mode_ref[at, 3 * f + k, block, rows, :] for k in range(3)] + [image_last_ref[at, f, block, rows, :]] for f in range(3)]
            for at in range(2)
        )
        face = load(face_mode_ref, 1)
        planes = [pick(first_core, load(face_mode_ref, 0), inner), pick(first_core, face, beyond), pick(first_core, inner, face)]
        low = planes[0]
        for x in range(2):
            high = planes[x + 1]
            total = total + mode_energy(element_modes(low, high), elem_ref[2 * core + x, block, rows, :])
            low = high
        return total

    energy = lax.fori_loop(0, 2 * tiles, energy_of, zeros(8, width), unroll=True)
    line = lax.broadcasted_iota(jnp.int32, (8, width), 0)
    packed = zeros(8, width)
    for k, value in enumerate((norm, cross, square, energy)):
        packed = jnp.where(line == k, jnp.sum(value, axis=0, keepdims=True), packed)
    sums_ref[...] = jnp.broadcast_to(packed[None], sums_ref.shape)


def stress_kernel(
    ends_ref, elem_ref, image_mode_ref, side_ref, give_ref, take_ref,
    late_ref, middle_ref, outer_mode_ref, face_mode_ref, part_ref, image_part_ref,
):
    core, slab = lax.axis_index("gy"), lax.axis_index("gx")
    cells, width = elem_ref.shape[2:]
    tiles = cells // 8
    count_last = jnp.where(slab == lax.axis_size("gx") - 1, 1.0, 0.5)
    zeros = lambda *dims: jnp.zeros(dims, jnp.float32)
    part_ref[:, :, :, cells : cells + 8, :] = zeros(2, 6, 2, 8, width)
    image_part_ref[:, :, :, cells : cells + 8, :] = zeros(4, 6, 2, 8, width)
    for f in range(3):
        for ref, mine in ((give_ref, core), (take_ref, 1 - core)):
            blocks = lambda base: [ref[base + f, block] for block in range(2)]
            store_modes(face_mode_ref, 3 * mine, f, blocks(0))
            store_modes(face_mode_ref, 1 + mine, f, blocks(3))
            store_modes(outer_mode_ref, 3 * mine, f, blocks(6))
        for i in range(2):
            store_modes(outer_mode_ref, 1 + i, f, [ends_ref[i, f, block] for block in range(2)])

    @pl.loop(0, 2 * tiles, unroll=True)
    def _(t):
        block, rows = t // tiles, pl.ds(pl.multiple_of((t % tiles) * 8, 8), 8)
        load = lambda ref, at, step=4: [[ref[at, step * f + k, block, rows, :] for k in range(3)] for f in range(3)]
        given, taken = give_ref[9, block, rows, :], take_ref[9, block, rows, :]
        modulus = [elem_ref[x, block, rows, :] for x in range(4)] + [jnp.where(core == 0, taken, given)]
        lower = mode_stress(load(outer_mode_ref, 0), load(outer_mode_ref, 1), modulus[0])
        upper = mode_stress(load(outer_mode_ref, 2), load(outer_mode_ref, 3), modulus[4])
        for k in range(6):
            part_ref[0, k, block, rows, :] = lower[k] + side_ref[0, k, block, rows, :]
            part_ref[1, k, block, rows, :] = side_ref[1, k, block, rows, :] + upper[k]
        planes = [(face_mode_ref, 0), (face_mode_ref, 1), (image_mode_ref, 0, 3), (image_mode_ref, 1, 3), (face_mode_ref, 2), (face_mode_ref, 3)]
        low, kept = load(*planes[0]), None
        for x in range(1, 6):
            high = load(*planes[x])
            now = mode_stress(low, high, modulus[x - 1])
            if kept is not None:
                for k in range(6):
                    image_part_ref[x - 2, k, block, rows, :] = kept[k] + now[k]
            low, kept = high, now

    for i in range(2):
        count = count_last if i else 0.5
        for k in range(6):
            late_ref[i, k] = nodal_average(part_ref, i, k, core, count)
            late_ref[i, 12 + k] = nodal_average(image_part_ref, 3 * i, k, core, count)
            middle_ref[i, k] = nodal_average(image_part_ref, 1 + i, k, core, 0.5)
        for f in range(3):
            late_ref[i, 6 + f] = jnp.where(core == i, give_ref[3 + f, core], take_ref[3 + f, core])
            late_ref[i, 9 + f] = ends_ref[i, f, core]


def combine_kernel(sums_ref, early_ref, late_ref, middle_ref, field_ref, stress_ref):
    total = jnp.sum(jnp.sum(sums_ref[...], axis=0), axis=1, keepdims=True)
    norm, cross, square, energy = (total[k : k + 1, :] for k in range(4))
    first = norm / cross
    norm_next = norm - 2.0 * first * cross + first * first * square
    ratio = norm_next / norm
    grown = 1.0 + ratio
    curvature = grown * grown * cross - 2.0 * grown * first * square + first * first * energy
    second = norm_next / curvature
    weight = jnp.broadcast_to(first + second * grown, early_ref.shape[2:])
    weight_image = jnp.broadcast_to(-second * first, early_ref.shape[2:])
    cells = early_ref.shape[2]
    for x in range(4):
        rows, i = pl.ds(x, cells, stride=4), (0, 0, 1, 1)[x]
        first_ref = late_ref if x in (0, 3) else early_ref
        for f in range(3):
            field_ref[f, rows, :] = weight * first_ref[i, 9 + f] + weight_image * first_ref[i, 6 + f]
        for k in range(6):
            image = late_ref[i, 12 + k] if x in (0, 3) else middle_ref[i, k]
            stress_ref[k, rows, :] = weight * first_ref[i, k] + weight_image * image


def cost(flops, size):
    return pl.CostEstimate(flops=flops, bytes_accessed=size, transcendentals=0)


def per_device(body_force, modulus):
    cells, planes, width = modulus.shape
    slabs, cores = lax.axis_size("gx"), lax.axis_size("gy")
    assert planes == 4 and cores == 2 and cells % 8 == 0
    both = ("gx", "gy")
    f32 = jnp.float32
    shape = lambda *dims: jax.ShapeDtypeStruct(dims, f32)
    scratch = lambda *dims: pltpu.VMEM(dims, f32)

    own, same, cross = pl.pallas_call(
        pack_kernel,
        out_shape=(shape(4, 4, cells, width), shape(2, 4, cells, width), shape(2, 4, cells, width)),
        in_specs=[pl.BlockSpec(memory_space=pl.ANY)] * 2,
        out_specs=[VMEM] * 3,
        scratch_shapes=[scratch(3, cells * 4, width), scratch(cells * 4, width), pltpu.SemaphoreType.DMA((2,))],
        compiler_params=LIMIT,
        name="pack",
    )(
        pltpu.with_memory_space_constraint(body_force.reshape(3, cells * 4, width), pltpu.HBM),
        pltpu.with_memory_space_constraint(modulus.reshape(cells * 4, width), pltpu.HBM),
    )

    up = [(2 * g, 2 * g + 2) for g in range(slabs - 1)]
    down = [(2 * g + 3, 2 * g + 1) for g in range(slabs - 1)]
    pairs = [(2 * g + 1, 2 * g + 2) for g in range(slabs - 1)]
    mate = lax.ppermute(own, "gy", [(0, 1), (1, 0)])
    cross_in = lax.ppermute(cross, both, pairs + [(q, p) for p, q in pairs])
    same_in = lax.ppermute(same, both, up + down)

    ends, elem, edge_part, part_sums, edge_mode, image_mode, image_last, side, early = pl.pallas_call(
        inner_kernel,
        out_shape=(
            shape(2, 3, 2, cells, width),
            shape(4, 2, cells, width),
            shape(12, 2, cells, width),
            shape(3, 8, width),
            shape(12, 2, cells, width),
            shape(2, 9, 2, cells, width),
            shape(2, 3, 2, cells, width),
            shape(2, 6, 2, cells, width),
            shape(2, 12, cells, width),
        ),
        in_specs=[VMEM] * 2,
        out_specs=[VMEM] * 9,
        scratch_shapes=[
            scratch(4, 3, 2, 8 + cells, width),
            scratch(4, 12, 2, cells, width),
            scratch(2, 12, 2, 8 + cells, width),
            scratch(2, 6, 2, 8 + cells, width),
        ],
        compiler_params=LIMIT,
        cost_estimate=cost(20_000_000, 4_000_000),
        name="inner",
    )(own, mate)
    give, sums = pl.pallas_call(
        outer_kernel,
        out_shape=(shape(10, 2, cells, width), shape(slabs * cores, 8, width)),
        in_specs=[VMEM] * 9,
        out_specs=[VMEM] * 2,
        scratch_shapes=[
            scratch(2, 12, 2, cells, width),
            scratch(2, 12, 2, cells, width),
            scratch(2, 12, 2, 8 + cells, width),
            scratch(2, 2, cells, width),
        ],
        compiler_params=LIMIT,
        cost_estimate=cost(10_000_000, 3_000_000),
        name="outer",
    )(ends, elem, edge_part, part_sums, edge_mode, image_mode, image_last, same_in, cross_in)

    take = lax.ppermute(give, "gy", [(0, 1), (1, 0)])
    sums = lax.all_to_all(sums, both, 0, 0, axis_index_groups=[list(range(slabs * cores))[::-1]])
    late, middle = pl.pallas_call(
        stress_kernel,
        out_shape=(shape(2, 18, cells, width), shape(2, 6, cells, width)),
        in_specs=[VMEM] * 6,
        out_specs=[VMEM] * 2,
        scratch_shapes=[
            scratch(4, 12, 2, cells, width),
            scratch(4, 12, 2, cells, width),
            scratch(2, 6, 2, 8 + cells, width),
            scratch(4, 6, 2, 8 + cells, width),
        ],
        compiler_params=LIMIT,
        cost_estimate=cost(20_000_000, 4_000_000),
        name="stress",
    )(ends, elem, image_mode, side, give, take)

    field, stress = pl.pallas_call(
        combine_kernel,
        out_shape=(shape(3, cells * 4, width), shape(6, cells * 4, width)),
        in_specs=[VMEM] * 4,
        out_specs=[VMEM] * 2,
        compiler_params=LIMIT,
        name="combine",
    )(sums, early, late, middle)
    return field.reshape(3, cells, 4, width), stress.reshape(6, cells, 4, width)


def solution(mesh):
    return jax.shard_map(
        per_device,
        mesh=mesh,
        in_specs=(P(None, "sample", "gx", "gy"), P("sample", "gx", "gy")),
        out_specs=(P(None, "sample", "gx", "gy"), P(None, "sample", "gx", "gy")),
        check_vma=False,
    )
```

```python
import functools

import jax
import jax.numpy as jnp
from jax import lax
from jax.experimental import pallas as pl
from jax.experimental.pallas import tpu as pltpu
from jax.sharding import PartitionSpec as P

POISSON = 0.3
LAME = POISSON / ((1.0 + POISSON) * (1.0 - 2.0 * POISSON))
SHEAR = 1.0 / (2.0 * (1.0 + POISSON))
RATIO = LAME / SHEAR
ONE = SHEAR / 16.0
TWO = SHEAR / 48.0
THREE = (LAME + 4.0 * SHEAR) / 144.0

VMEM = pl.BlockSpec(memory_space=pltpu.VMEM)
LIMIT = pltpu.CompilerParams(vmem_limit_bytes=48 << 20)


def lanes(shape):
    return lax.broadcasted_iota(jnp.int32, shape, len(shape) - 1)


def from_left(first, second):
    edge = lanes(first.shape) == 0
    turned, turned2 = pltpu.roll(first, 1, 1), pltpu.roll(second, 1, 1)
    return jnp.where(edge, 0.0, turned), jnp.where(edge, turned, turned2)


def from_right(first, second):
    edge = lanes(first.shape) == first.shape[1] - 1
    turned, turned2 = (pltpu.roll(v, v.shape[1] - 1, 1) for v in (first, second))
    return jnp.where(edge, turned2, turned), jnp.where(edge, 0.0, turned2)


def pack_kernel(force_hbm, modulus_hbm, own_ref, same_ref, cross_ref, force_ref, modulus_ref, sem):
    core = lax.axis_index("gy")
    cells = own_ref.shape[2]
    copies = [
        pltpu.make_async_copy(force_hbm, force_ref, sem.at[0]),
        pltpu.make_async_copy(modulus_hbm, modulus_ref, sem.at[1]),
    ]
    for copy in copies:
        copy.start()
    for copy in copies:
        copy.wait()

    def plane(field, x):
        rows = pl.ds(x, cells, stride=4)
        return force_ref[field, rows, :] if field < 3 else modulus_ref[rows, :]

    for field in range(4):
        for x in range(4):
            own_ref[x, field] = plane(field, x)
        for i in range(2):
            same_ref[i, field] = plane(field, 2 * (1 - core) + i)
            cross_ref[i, field] = plane(field, 2 * core + i)


def below(value):
    row = lax.broadcasted_iota(jnp.int32, value.shape, 0)
    return jnp.where(row == 0, 0.0, pltpu.roll(value, 1, 0))


def store_modes(mode_ref, at, field, high, low=None, last_ref=None):
    base = 4 * field if last_ref is None else 3 * field
    left = from_left(*high)
    for block in range(2):
        value, beside = high[block], left[block]
        value_low = below(value) if low is None else low[block]
        beside_low = below(beside)
        total, total_beside = value + value_low, beside + beside_low
        slope, slope_beside = value - value_low, beside - beside_low
        mode_ref[at, base, block] = total + total_beside
        mode_ref[at, base + 1, block] = slope + slope_beside
        mode_ref[at, base + 2, block] = total - total_beside
        if last_ref is None:
            mode_ref[at, base + 3, block] = slope - slope_beside
        else:
            last_ref[at, field, block] = slope - slope_beside


def element_modes(low, high):
    found = []
    for component in range(3):
        modes = {}
        for kind, (z, y) in enumerate(((0, 0), (1, 0), (0, 1), (1, 1))):
            lo, hi = low[component][kind], high[component][kind]
            if (z, y) != (0, 0):
                modes[z, 0, y] = hi + lo
            modes[z, 1, y] = hi - lo
        found.append(modes)
    return found


def mode_forces(modes, modulus):
    u, v, w = modes
    one, two, three = modulus * ONE, modulus * TWO, modulus * THREE
    trace = RATIO * (u[1, 0, 0] + v[0, 1, 0] + w[0, 0, 1])
    shear_zx = one * (u[0, 1, 0] + v[1, 0, 0])
    shear_xy = one * (v[0, 0, 1] + w[0, 1, 0])
    shear_zy = one * (u[0, 0, 1] + w[1, 0, 0])
    trace_z = RATIO * (v[1, 1, 0] + w[1, 0, 1])
    trace_x = RATIO * (u[1, 1, 0] + w[0, 1, 1])
    trace_y = RATIO * (u[1, 0, 1] + v[0, 1, 1])
    mixed_zx = u[0, 1, 1] + v[1, 0, 1]
    mixed_xy = v[1, 0, 1] + w[1, 1, 0]
    mixed_zy = u[0, 1, 1] + w[1, 1, 0]
    return (
        {
            (1, 0, 0): one * (trace + 2.0 * u[1, 0, 0]),
            (0, 1, 0): shear_zx,
            (0, 0, 1): shear_zy,
            (1, 1, 0): two * (trace_x + 3.0 * u[1, 1, 0]),
            (1, 0, 1): two * (trace_y + 3.0 * u[1, 0, 1]),
            (0, 1, 1): two * (mixed_zx + mixed_zy),
            (1, 1, 1): three * u[1, 1, 1],
        },
        {
            (0, 1, 0): one * (trace + 2.0 * v[0, 1, 0]),
            (1, 0, 0): shear_zx,
            (0, 0, 1): shear_xy,
            (1, 1, 0): two * (trace_z + 3.0 * v[1, 1, 0]),
            (0, 1, 1): two * (trace_y + 3.0 * v[0, 1, 1]),
            (1, 0, 1): two * (mixed_zx + mixed_xy),
            (1, 1, 1): three * v[1, 1, 1],
        },
        {
            (0, 0, 1): one * (trace + 2.0 * w[0, 0, 1]),
            (1, 0, 0): shear_zy,
            (0, 1, 0): shear_xy,
            (1, 0, 1): two * (trace_z + 3.0 * w[1, 0, 1]),
            (0, 1, 1): two * (trace_x + 3.0 * w[0, 1, 1]),
            (1, 1, 0): two * (mixed_xy + mixed_zy),
            (1, 1, 1): three * w[1, 1, 1],
        },
    )


def mode_energy(modes, modulus):
    u, v, w = modes
    square = lambda value: value * value
    a, b, c = u[1, 0, 0], v[0, 1, 0], w[0, 0, 1]
    one = RATIO * square(a + b + c) + 2.0 * (square(a) + square(b) + square(c))
    one = one + square(u[0, 1, 0] + v[1, 0, 0]) + square(v[0, 0, 1] + w[0, 1, 0]) + square(u[0, 0, 1] + w[1, 0, 0])
    d, e, f = u[1, 1, 0], u[1, 0, 1], v[1, 1, 0]
    g, h, k = v[0, 1, 1], w[1, 0, 1], w[0, 1, 1]
    two = RATIO * (square(f + h) + square(d + k) + square(e + g))
    two = two + 3.0 * (square(d) + square(e) + square(f) + square(g) + square(h) + square(k))
    m, n, o = u[0, 1, 1], v[1, 0, 1], w[1, 1, 0]
    two = two + square(m + n) + square(n + o) + square(m + o)
    three = square(u[1, 1, 1]) + square(v[1, 1, 1]) + square(w[1, 1, 1])
    return modulus * (ONE * one + TWO * two + THREE * three)


def face_forces(forces):
    upper, lower = [], []
    for component in range(3):
        up, down = [], []
        for z, y in ((0, 0), (1, 0), (0, 1), (1, 1)):
            diff, both = forces[component][z, 1, y], forces[component].get((z, 0, y))
            up.append(diff if both is None else both + diff)
            down.append(-diff if both is None else both - diff)
        upper.append(up)
        lower.append(down)
    return upper, lower


def corner_forces(modes):
    ss, ds, sd, dd = modes
    here, back = ss + ds, ss - ds
    here_y, back_y = sd + dd, sd - dd
    return here + here_y, here - here_y, back + back_y, back - back_y


def plus(first, second):
    return [[p + q for p, q in zip(a, b)] for a, b in zip(first, second)]


def pick(flag, first, second):
    return [[jnp.where(flag, p, q) for p, q in zip(a, b)] for a, b in zip(first, second)]


def assembled(part_ref, at, field, cells):
    here = lambda k, block: part_ref[at, 4 * field + k, block, 0:cells, :]
    above = lambda k, block: part_ref[at, 4 * field + k, block, 1 : cells + 1, :]
    beside = from_right(*(here(1, block) + above(3, block) for block in range(2)))
    return [here(0, block) + above(2, block) + beside[block] for block in range(2)]


def mode_stress(low, high, modulus):
    by_z = [high[f][1] + low[f][1] for f in range(3)]
    by_x = [high[f][0] - low[f][0] for f in range(3)]
    by_y = [high[f][2] + low[f][2] for f in range(3)]
    scaled = modulus * (0.25 * SHEAR)
    trace = RATIO * (by_z[0] + by_x[1] + by_y[2])
    return [
        scaled * (trace + 2.0 * by_z[0]),
        scaled * (trace + 2.0 * by_x[1]),
        scaled * (trace + 2.0 * by_y[2]),
        scaled * (by_x[0] + by_z[1]),
        scaled * (by_y[1] + by_x[2]),
        scaled * (by_y[0] + by_z[2]),
    ]


def nodal_average(part_ref, at, k, core, count_x):
    cells, width = part_ref.shape[3] - 8, part_ref.shape[4]
    both = [part_ref[at, k, block, 0:cells, :] + part_ref[at, k, block, 1 : cells + 1, :] for block in range(2)]
    first, second = both
    lane = lanes((cells, width))
    row = lax.broadcasted_iota(jnp.int32, (cells, width), 0)
    mine = jnp.where(core == 0, first, second)
    turned = pltpu.roll(jnp.where(lane == 0, jnp.where(core == 0, second, 0.0), mine), width - 1, 1)
    count = jnp.where(row == cells - 1, 1.0, 0.5) * jnp.where((lane == width - 1) & (core == 1), 1.0, 0.5)
    return (mine + turned) * (count * count_x)


def inner_kernel(
    own_ref, mate_ref, _arrived, ends_ref, elem_ref, edge_part_ref, sums_ref, edge_mode_ref, image_mode_ref, image_last_ref, side_ref, early_ref,
    node_ref, mode_ref, part_ref, stress_part_ref,
):
    core = lax.axis_index("gy")
    cells, width = own_ref.shape[2:]
    tiles = cells // 8
    zeros = lambda *dims: jnp.zeros(dims, jnp.float32)
    node_ref[:, :, :, 0:8, :] = zeros(4, 3, 2, 8, width)
    for x in range(4):
        for ref, block in ((own_ref, core), (mate_ref, 1 - core)):
            for field in range(3):
                node_ref[x, field, block, 8 : 8 + cells, :] = ref[x, field]
                if x in (0, 3):
                    ends_ref[x // 3, field, block] = ref[x, field]
            elem_ref[x, block] = ref[x, 3]

    @pl.loop(0, 4)
    def _(x):
        for field in range(3):
            high, low = ([node_ref[x, field, block, at : at + cells, :] for block in range(2)] for at in (8, 7))
            store_modes(mode_ref, x, field, high, low)

    edge_mode_ref[...] = mode_ref[3 * core]
    part_ref[:, :, :, cells : cells + 8, :] = zeros(2, 12, 2, 8, width)
    stress_part_ref[:, :, :, cells : cells + 8, :] = zeros(2, 6, 2, 8, width)

    @pl.loop(0, 2 * tiles, unroll=True)
    def _(t):
        block, rows = t // tiles, pl.ds(pl.multiple_of((t % tiles) * 8, 8), 8)
        load = lambda x: [[mode_ref[x, 4 * f + k, block, rows, :] for k in range(4)] for f in range(3)]
        low, kept, outer = load(0), None, None
        for x in range(1, 4):
            high = load(x)
            upper, lower = face_forces(mode_forces(element_modes(low, high), elem_ref[x, block, rows, :]))
            if kept is None:
                outer = lower
            else:
                for f, modes in enumerate(plus(kept, lower)):
                    for k, value in enumerate(corner_forces(modes)):
                        part_ref[x - 2, 4 * f + k, block, rows, :] = value
            low, kept = high, upper
        for f in range(3):
            for k in range(4):
                edge_part_ref[4 * f + k, block, rows, :] = jnp.where(core == 0, outer[f][k], kept[f][k])

    @pl.loop(0, 2 * tiles, unroll=True)
    def _(t):
        block, rows = t // tiles, pl.ds(pl.multiple_of((t % tiles) * 8, 8), 8)
        load = lambda x: [[mode_ref[x, 4 * f + k, block, rows, :] for k in range(3)] for f in range(3)]
        low, kept = load(0), None
        for x in range(1, 4):
            high = load(x)
            now = mode_stress(low, high, elem_ref[x, block, rows, :])
            for k in range(6):
                if x > 1:
                    stress_part_ref[x - 2, k, block, rows, :] = kept[k] + now[k]
                if x != 2:
                    side_ref[x // 2, k, block, rows, :] = now[k]
            low, kept = high, now

    fold = lambda value: value.reshape(tiles, 8, width).sum(0)
    norm = cross = square = zeros(8, width)
    for i in range(2):
        mine = jnp.where(core == i, 1.0, 0.0)
        for f in range(3):
            values = assembled(part_ref, i, f, cells)
            store_modes(image_mode_ref, i, f, values, last_ref=image_last_ref)
            early_ref[i, 6 + f] = jnp.where(core == 0, values[0], values[1])
            early_ref[i, 9 + f] = own_ref[1 + i, f]
            for block, value in enumerate(values):
                force = node_ref[i + 1, f, block, 8 : 8 + cells, :]
                norm = norm + mine * fold(force * force)
                cross = cross + mine * fold(force * value)
                square = square + mine * fold(value * value)
        for k in range(6):
            early_ref[i, k] = nodal_average(stress_part_ref, i, k, core, 0.5)
    for k, value in enumerate((norm, cross, square)):
        sums_ref[k] = value


def outer_kernel(
    ends_ref, elem_ref, edge_part_ref, part_sums_ref, edge_mode_ref, image_mode_ref, image_last_ref, same_ref, cross_ref,
    give_ref, sums_ref, halo_mode_ref, face_mode_ref, part_ref, halo_elem_ref,
):
    core, slab = lax.axis_index("gy"), lax.axis_index("gx")
    cells, width = same_ref.shape[2:]
    tiles = cells // 8
    zeros = lambda *dims: jnp.zeros(dims, jnp.float32)
    near = 1 - core
    first_core = core == 0
    for i in range(2):
        for f in range(4):
            same, cross = same_ref[i, f], cross_ref[i, f]
            values = [jnp.where(first_core, same, cross), jnp.where(first_core, cross, same)]
            if f < 3:
                store_modes(halo_mode_ref, i, f, values)
            else:
                halo_elem_ref[i, 0], halo_elem_ref[i, 1] = values
    for f in range(4):
        give_ref[6 + f, core] = same_ref[near, f]
        give_ref[6 + f, near] = cross_ref[near, f]

    part_ref[:, :, :, cells : cells + 8, :] = zeros(2, 12, 2, 8, width)

    @pl.loop(0, 2 * tiles, unroll=True)
    def _(t):
        block, rows = t // tiles, pl.ds(pl.multiple_of((t % tiles) * 8, 8), 8)
        load = lambda at: [[halo_mode_ref[at, 4 * f + k, block, rows, :] for k in range(4)] for f in range(3)]
        edge = [[edge_mode_ref[4 * f + k, block, rows, :] for k in range(4)] for f in range(3)]
        halo = [load(0), load(1)]
        planes = [pick(first_core, halo[0], edge), pick(first_core, halo[1], halo[0]), pick(first_core, edge, halo[1])]
        first = halo_elem_ref[near, block, rows, :]
        second = jnp.where(first_core, elem_ref[0, block, rows, :], halo_elem_ref[1, block, rows, :])
        upper, lower = face_forces(mode_forces(element_modes(planes[0], planes[1]), first))
        upper2, lower2 = face_forces(mode_forces(element_modes(planes[1], planes[2]), second))
        for f, modes in enumerate(plus(upper, lower2)):
            for k, value in enumerate(corner_forces(modes)):
                part_ref[0, 4 * f + k, block, rows, :] = value
        for f in range(3):
            modes = [edge_part_ref[4 * f + k, block, rows, :] + jnp.where(first_core, upper2[f][k], lower[f][k]) for k in range(4)]
            for k, value in enumerate(corner_forces(modes)):
                part_ref[1, 4 * f + k, block, rows, :] = value

    clamped = jnp.where(first_core & (slab == 0), 0.0, 1.0)
    fold = lambda value: value.reshape(tiles, 8, width).sum(0)
    norm, cross, square = (part_sums_ref[k] for k in range(3))
    for f in range(3):
        values = [value * clamped for value in assembled(part_ref, 0, f, cells)]
        store_modes(face_mode_ref, 0, f, values)
        for block in range(2):
            give_ref[f, block] = values[block]
        values = assembled(part_ref, 1, f, cells)
        store_modes(face_mode_ref, 1, f, values)
        for block, value in enumerate(values):
            give_ref[3 + f, block] = value
            force = ends_ref[core, f, block]
            norm = norm + fold(force * force)
            cross = cross + fold(force * value)
            square = square + fold(value * value)

    def energy_of(t, total):
        block, rows = t // tiles, pl.ds(pl.multiple_of((t % tiles) * 8, 8), 8)
        load = lambda ref, at: [[ref[at, 4 * f + k, block, rows, :] for k in range(4)] for f in range(3)]
        inner, beyond = (
            [[image_mode_ref[at, 3 * f + k, block, rows, :] for k in range(3)] + [image_last_ref[at, f, block, rows, :]] for f in range(3)]
            for at in range(2)
        )
        face = load(face_mode_ref, 1)
        planes = [pick(first_core, load(face_mode_ref, 0), inner), pick(first_core, face, beyond), pick(first_core, inner, face)]
        low = planes[0]
        for x in range(2):
            high = planes[x + 1]
            total = total + mode_energy(element_modes(low, high), elem_ref[2 * core + x, block, rows, :])
            low = high
        return total

    energy = lax.fori_loop(0, 2 * tiles, energy_of, zeros(8, width), unroll=True)
    line = lax.broadcasted_iota(jnp.int32, (8, width), 0)
    packed = zeros(8, width)
    for k, value in enumerate((norm, cross, square, energy)):
        packed = jnp.where(line == k, jnp.sum(value, axis=0, keepdims=True), packed)
    sums_ref[...] = jnp.broadcast_to(packed[None], sums_ref.shape)


def stress_kernel(
    ends_ref, elem_ref, image_mode_ref, side_ref, give_ref, take_ref,
    late_ref, middle_ref, outer_mode_ref, face_mode_ref, part_ref, image_part_ref,
):
    core, slab = lax.axis_index("gy"), lax.axis_index("gx")
    cells, width = elem_ref.shape[2:]
    tiles = cells // 8
    count_last = jnp.where(slab == lax.axis_size("gx") - 1, 1.0, 0.5)
    zeros = lambda *dims: jnp.zeros(dims, jnp.float32)
    part_ref[:, :, :, cells : cells + 8, :] = zeros(2, 6, 2, 8, width)
    image_part_ref[:, :, :, cells : cells + 8, :] = zeros(4, 6, 2, 8, width)
    for f in range(3):
        for ref, mine in ((give_ref, core), (take_ref, 1 - core)):
            blocks = lambda base: [ref[base + f, block] for block in range(2)]
            store_modes(face_mode_ref, 3 * mine, f, blocks(0))
            store_modes(face_mode_ref, 1 + mine, f, blocks(3))
            store_modes(outer_mode_ref, 3 * mine, f, blocks(6))
        for i in range(2):
            store_modes(outer_mode_ref, 1 + i, f, [ends_ref[i, f, block] for block in range(2)])

    @pl.loop(0, 2 * tiles, unroll=True)
    def _(t):
        block, rows = t // tiles, pl.ds(pl.multiple_of((t % tiles) * 8, 8), 8)
        load = lambda ref, at, step=4: [[ref[at, step * f + k, block, rows, :] for k in range(3)] for f in range(3)]
        given, taken = give_ref[9, block, rows, :], take_ref[9, block, rows, :]
        modulus = [elem_ref[x, block, rows, :] for x in range(4)] + [jnp.where(core == 0, taken, given)]
        lower = mode_stress(load(outer_mode_ref, 0), load(outer_mode_ref, 1), modulus[0])
        upper = mode_stress(load(outer_mode_ref, 2), load(outer_mode_ref, 3), modulus[4])
        for k in range(6):
            part_ref[0, k, block, rows, :] = lower[k] + side_ref[0, k, block, rows, :]
            part_ref[1, k, block, rows, :] = side_ref[1, k, block, rows, :] + upper[k]
        planes = [(face_mode_ref, 0), (face_mode_ref, 1), (image_mode_ref, 0, 3), (image_mode_ref, 1, 3), (face_mode_ref, 2), (face_mode_ref, 3)]
        low, kept = load(*planes[0]), None
        for x in range(1, 6):
            high = load(*planes[x])
            now = mode_stress(low, high, modulus[x - 1])
            if kept is not None:
                for k in range(6):
                    image_part_ref[x - 2, k, block, rows, :] = kept[k] + now[k]
            low, kept = high, now

    for i in range(2):
        count = count_last if i else 0.5
        for k in range(6):
            late_ref[i, k] = nodal_average(part_ref, i, k, core, count)
            late_ref[i, 12 + k] = nodal_average(image_part_ref, 3 * i, k, core, count)
            middle_ref[i, k] = nodal_average(image_part_ref, 1 + i, k, core, 0.5)
        for f in range(3):
            late_ref[i, 6 + f] = jnp.where(core == i, give_ref[3 + f, core], take_ref[3 + f, core])
            late_ref[i, 9 + f] = ends_ref[i, f, core]


def combine_kernel(sums_ref, early_ref, late_ref, middle_ref, field_ref, stress_ref):
    total = jnp.sum(jnp.sum(sums_ref[...], axis=0), axis=1, keepdims=True)
    norm, cross, square, energy = (total[k : k + 1, :] for k in range(4))
    first = norm / cross
    norm_next = norm - 2.0 * first * cross + first * first * square
    ratio = norm_next / norm
    grown = 1.0 + ratio
    curvature = grown * grown * cross - 2.0 * grown * first * square + first * first * energy
    second = norm_next / curvature
    weight = jnp.broadcast_to(first + second * grown, early_ref.shape[2:])
    weight_image = jnp.broadcast_to(-second * first, early_ref.shape[2:])
    cells = early_ref.shape[2]
    for x in range(4):
        rows, i = pl.ds(x, cells, stride=4), (0, 0, 1, 1)[x]
        first_ref = late_ref if x in (0, 3) else early_ref
        for f in range(3):
            field_ref[f, rows, :] = weight * first_ref[i, 9 + f] + weight_image * first_ref[i, 6 + f]
        for k in range(6):
            image = late_ref[i, 12 + k] if x in (0, 3) else middle_ref[i, k]
            stress_ref[k, rows, :] = weight * first_ref[i, k] + weight_image * image


def cost(flops, size):
    return pl.CostEstimate(flops=flops, bytes_accessed=size, transcendentals=0)


def per_device(body_force, modulus):
    cells, planes, width = modulus.shape
    slabs, cores = lax.axis_size("gx"), lax.axis_size("gy")
    assert planes == 4 and cores == 2 and cells % 8 == 0
    both = ("gx", "gy")
    f32 = jnp.float32
    shape = lambda *dims: jax.ShapeDtypeStruct(dims, f32)
    scratch = lambda *dims: pltpu.VMEM(dims, f32)

    own, same, cross = pl.pallas_call(
        pack_kernel,
        out_shape=(shape(4, 4, cells, width), shape(2, 4, cells, width), shape(2, 4, cells, width)),
        in_specs=[pl.BlockSpec(memory_space=pl.ANY)] * 2,
        out_specs=[VMEM] * 3,
        scratch_shapes=[scratch(3, cells * 4, width), scratch(cells * 4, width), pltpu.SemaphoreType.DMA((2,))],
        compiler_params=LIMIT,
        name="pack",
    )(
        pltpu.with_memory_space_constraint(body_force.reshape(3, cells * 4, width), pltpu.HBM),
        pltpu.with_memory_space_constraint(modulus.reshape(cells * 4, width), pltpu.HBM),
    )

    up = [(2 * g, 2 * g + 2) for g in range(slabs - 1)]
    down = [(2 * g + 3, 2 * g + 1) for g in range(slabs - 1)]
    pairs = [(2 * g + 1, 2 * g + 2) for g in range(slabs - 1)]
    mate = lax.ppermute(own, "gy", [(0, 1), (1, 0)])
    cross_in = lax.ppermute(cross, both, pairs + [(q, p) for p, q in pairs])
    same_in = lax.ppermute(same, both, up + down)

    ends, elem, edge_part, part_sums, edge_mode, image_mode, image_last, side, early = pl.pallas_call(
        inner_kernel,
        out_shape=(
            shape(2, 3, 2, cells, width),
            shape(4, 2, cells, width),
            shape(12, 2, cells, width),
            shape(3, 8, width),
            shape(12, 2, cells, width),
            shape(2, 9, 2, cells, width),
            shape(2, 3, 2, cells, width),
            shape(2, 6, 2, cells, width),
            shape(2, 12, cells, width),
        ),
        in_specs=[VMEM] * 2 + [pl.BlockSpec(memory_space=pl.ANY)],
        out_specs=[VMEM] * 9,
        scratch_shapes=[
            scratch(4, 3, 2, 8 + cells, width),
            scratch(4, 12, 2, cells, width),
            scratch(2, 12, 2, 8 + cells, width),
            scratch(2, 6, 2, 8 + cells, width),
        ],
        compiler_params=LIMIT,
        cost_estimate=cost(20_000_000, 4_000_000),
        name="inner",
    )(own, mate, cross_in)
    give, sums = pl.pallas_call(
        outer_kernel,
        out_shape=(shape(10, 2, cells, width), shape(slabs * cores, 8, width)),
        in_specs=[VMEM] * 9,
        out_specs=[VMEM] * 2,
        scratch_shapes=[
            scratch(2, 12, 2, cells, width),
            scratch(2, 12, 2, cells, width),
            scratch(2, 12, 2, 8 + cells, width),
            scratch(2, 2, cells, width),
        ],
        compiler_params=LIMIT,
        cost_estimate=cost(10_000_000, 3_000_000),
        name="outer",
    )(ends, elem, edge_part, part_sums, edge_mode, image_mode, image_last, same_in, cross_in)

    take = lax.ppermute(give, "gy", [(0, 1), (1, 0)])
    sums = lax.all_to_all(sums, both, 0, 0, axis_index_groups=[list(range(slabs * cores))[::-1]])
    late, middle = pl.pallas_call(
        stress_kernel,
        out_shape=(shape(2, 18, cells, width), shape(2, 6, cells, width)),
        in_specs=[VMEM] * 6,
        out_specs=[VMEM] * 2,
        scratch_shapes=[
            scratch(4, 12, 2, cells, width),
            scratch(4, 12, 2, cells, width),
            scratch(2, 6, 2, 8 + cells, width),
            scratch(4, 6, 2, 8 + cells, width),
        ],
        compiler_params=LIMIT,
        cost_estimate=cost(20_000_000, 4_000_000),
        name="stress",
    )(ends, elem, image_mode, side, give, take)

    field, stress = pl.pallas_call(
        combine_kernel,
        out_shape=(shape(3, cells * 4, width), shape(6, cells * 4, width)),
        in_specs=[VMEM] * 4,
        out_specs=[VMEM] * 2,
        compiler_params=LIMIT,
        name="combine",
    )(sums, early, late, middle)
    return field.reshape(3, cells, 4, width), stress.reshape(6, cells, 4, width)


def solution(mesh):
    return jax.shard_map(
        per_device,
        mesh=mesh,
        in_specs=(P(None, "sample", "gx", "gy"), P("sample", "gx", "gy")),
        out_specs=(P(None, "sample", "gx", "gy"), P(None, "sample", "gx", "gy")),
        check_vma=False,
    )
```

```python
import functools

import jax
import jax.numpy as jnp
from jax import lax
from jax.experimental import pallas as pl
from jax.experimental.pallas import tpu as pltpu
from jax.sharding import PartitionSpec as P

POISSON = 0.3
LAME = POISSON / ((1.0 + POISSON) * (1.0 - 2.0 * POISSON))
SHEAR = 1.0 / (2.0 * (1.0 + POISSON))
RATIO = LAME / SHEAR
ONE = SHEAR / 16.0
TWO = SHEAR / 48.0
THREE = (LAME + 4.0 * SHEAR) / 144.0

VMEM = pl.BlockSpec(memory_space=pltpu.VMEM)
LIMIT = pltpu.CompilerParams(vmem_limit_bytes=48 << 20)


def lanes(shape):
    return lax.broadcasted_iota(jnp.int32, shape, len(shape) - 1)


def from_left(first, second):
    edge = lanes(first.shape) == 0
    turned, turned2 = pltpu.roll(first, 1, 1), pltpu.roll(second, 1, 1)
    return jnp.where(edge, 0.0, turned), jnp.where(edge, turned, turned2)


def from_right(first, second):
    edge = lanes(first.shape) == first.shape[1] - 1
    turned, turned2 = (pltpu.roll(v, v.shape[1] - 1, 1) for v in (first, second))
    return jnp.where(edge, turned2, turned), jnp.where(edge, 0.0, turned2)


def pack_kernel(force_hbm, modulus_hbm, own_ref, same_ref, cross_ref, force_ref, modulus_ref, sem):
    core = lax.axis_index("gy")
    cells = own_ref.shape[2]
    copies = [
        pltpu.make_async_copy(force_hbm, force_ref, sem.at[0]),
        pltpu.make_async_copy(modulus_hbm, modulus_ref, sem.at[1]),
    ]
    for copy in copies:
        copy.start()
    for copy in copies:
        copy.wait()

    def plane(field, x):
        rows = pl.ds(x, cells, stride=4)
        return force_ref[field, rows, :] if field < 3 else modulus_ref[rows, :]

    for field in range(4):
        for x in range(4):
            own_ref[x, field] = plane(field, x)
        for i in range(2):
            same_ref[i, field] = plane(field, 2 * (1 - core) + i)
            cross_ref[i, field] = plane(field, 2 * core + i)


def below(value):
    row = lax.broadcasted_iota(jnp.int32, value.shape, 0)
    return jnp.where(row == 0, 0.0, pltpu.roll(value, 1, 0))


def store_modes(mode_ref, at, field, high, low=None, last_ref=None):
    base = 4 * field if last_ref is None else 3 * field
    left = from_left(*high)
    for block in range(2):
        value, beside = high[block], left[block]
        value_low = below(value) if low is None else low[block]
        beside_low = below(beside)
        total, total_beside = value + value_low, beside + beside_low
        slope, slope_beside = value - value_low, beside - beside_low
        mode_ref[at, base, block] = total + total_beside
        mode_ref[at, base + 1, block] = slope + slope_beside
        mode_ref[at, base + 2, block] = total - total_beside
        if last_ref is None:
            mode_ref[at, base + 3, block] = slope - slope_beside
        else:
            last_ref[at, field, block] = slope - slope_beside


def element_modes(low, high):
    found = []
    for component in range(3):
        modes = {}
        for kind, (z, y) in enumerate(((0, 0), (1, 0), (0, 1), (1, 1))):
            lo, hi = low[component][kind], high[component][kind]
            if (z, y) != (0, 0):
                modes[z, 0, y] = hi + lo
            modes[z, 1, y] = hi - lo
        found.append(modes)
    return found


def mode_forces(modes, modulus):
    u, v, w = modes
    one, two, three = modulus * ONE, modulus * TWO, modulus * THREE
    trace = RATIO * (u[1, 0, 0] + v[0, 1, 0] + w[0, 0, 1])
    shear_zx = one * (u[0, 1, 0] + v[1, 0, 0])
    shear_xy = one * (v[0, 0, 1] + w[0, 1, 0])
    shear_zy = one * (u[0, 0, 1] + w[1, 0, 0])
    trace_z = RATIO * (v[1, 1, 0] + w[1, 0, 1])
    trace_x = RATIO * (u[1, 1, 0] + w[0, 1, 1])
    trace_y = RATIO * (u[1, 0, 1] + v[0, 1, 1])
    mixed_zx = u[0, 1, 1] + v[1, 0, 1]
    mixed_xy = v[1, 0, 1] + w[1, 1, 0]
    mixed_zy = u[0, 1, 1] + w[1, 1, 0]
    return (
        {
            (1, 0, 0): one * (trace + 2.0 * u[1, 0, 0]),
            (0, 1, 0): shear_zx,
            (0, 0, 1): shear_zy,
            (1, 1, 0): two * (trace_x + 3.0 * u[1, 1, 0]),
            (1, 0, 1): two * (trace_y + 3.0 * u[1, 0, 1]),
            (0, 1, 1): two * (mixed_zx + mixed_zy),
            (1, 1, 1): three * u[1, 1, 1],
        },
        {
            (0, 1, 0): one * (trace + 2.0 * v[0, 1, 0]),
            (1, 0, 0): shear_zx,
            (0, 0, 1): shear_xy,
            (1, 1, 0): two * (trace_z + 3.0 * v[1, 1, 0]),
            (0, 1, 1): two * (trace_y + 3.0 * v[0, 1, 1]),
            (1, 0, 1): two * (mixed_zx + mixed_xy),
            (1, 1, 1): three * v[1, 1, 1],
        },
        {
            (0, 0, 1): one * (trace + 2.0 * w[0, 0, 1]),
            (1, 0, 0): shear_zy,
            (0, 1, 0): shear_xy,
            (1, 0, 1): two * (trace_z + 3.0 * w[1, 0, 1]),
            (0, 1, 1): two * (trace_x + 3.0 * w[0, 1, 1]),
            (1, 1, 0): two * (mixed_xy + mixed_zy),
            (1, 1, 1): three * w[1, 1, 1],
        },
    )


def mode_energy(modes, modulus):
    u, v, w = modes
    square = lambda value: value * value
    a, b, c = u[1, 0, 0], v[0, 1, 0], w[0, 0, 1]
    one = RATIO * square(a + b + c) + 2.0 * (square(a) + square(b) + square(c))
    one = one + square(u[0, 1, 0] + v[1, 0, 0]) + square(v[0, 0, 1] + w[0, 1, 0]) + square(u[0, 0, 1] + w[1, 0, 0])
    d, e, f = u[1, 1, 0], u[1, 0, 1], v[1, 1, 0]
    g, h, k = v[0, 1, 1], w[1, 0, 1], w[0, 1, 1]
    two = RATIO * (square(f + h) + square(d + k) + square(e + g))
    two = two + 3.0 * (square(d) + square(e) + square(f) + square(g) + square(h) + square(k))
    m, n, o = u[0, 1, 1], v[1, 0, 1], w[1, 1, 0]
    two = two + square(m + n) + square(n + o) + square(m + o)
    three = square(u[1, 1, 1]) + square(v[1, 1, 1]) + square(w[1, 1, 1])
    return modulus * (ONE * one + TWO * two + THREE * three)


def face_forces(forces):
    upper, lower = [], []
    for component in range(3):
        up, down = [], []
        for z, y in ((0, 0), (1, 0), (0, 1), (1, 1)):
            diff, both = forces[component][z, 1, y], forces[component].get((z, 0, y))
            up.append(diff if both is None else both + diff)
            down.append(-diff if both is None else both - diff)
        upper.append(up)
        lower.append(down)
    return upper, lower


def corner_forces(modes):
    ss, ds, sd, dd = modes
    here, back = ss + ds, ss - ds
    here_y, back_y = sd + dd, sd - dd
    return here + here_y, here - here_y, back + back_y, back - back_y


def plus(first, second):
    return [[p + q for p, q in zip(a, b)] for a, b in zip(first, second)]


def pick(flag, first, second):
    return [[jnp.where(flag, p, q) for p, q in zip(a, b)] for a, b in zip(first, second)]


def assembled(part_ref, at, field, cells):
    here = lambda k, block: part_ref[at, 4 * field + k, block, 0:cells, :]
    above = lambda k, block: part_ref[at, 4 * field + k, block, 1 : cells + 1, :]
    beside = from_right(*(here(1, block) + above(3, block) for block in range(2)))
    return [here(0, block) + above(2, block) + beside[block] for block in range(2)]


def mode_stress(low, high, modulus):
    by_z = [high[f][1] + low[f][1] for f in range(3)]
    by_x = [high[f][0] - low[f][0] for f in range(3)]
    by_y = [high[f][2] + low[f][2] for f in range(3)]
    scaled = modulus * (0.25 * SHEAR)
    trace = RATIO * (by_z[0] + by_x[1] + by_y[2])
    return [
        scaled * (trace + 2.0 * by_z[0]),
        scaled * (trace + 2.0 * by_x[1]),
        scaled * (trace + 2.0 * by_y[2]),
        scaled * (by_x[0] + by_z[1]),
        scaled * (by_y[1] + by_x[2]),
        scaled * (by_y[0] + by_z[2]),
    ]


def nodal_average(part_ref, at, k, core, count_x):
    cells, width = part_ref.shape[3] - 8, part_ref.shape[4]
    both = [part_ref[at, k, block, 0:cells, :] + part_ref[at, k, block, 1 : cells + 1, :] for block in range(2)]
    first, second = both
    lane = lanes((cells, width))
    row = lax.broadcasted_iota(jnp.int32, (cells, width), 0)
    mine = jnp.where(core == 0, first, second)
    turned = pltpu.roll(jnp.where(lane == 0, jnp.where(core == 0, second, 0.0), mine), width - 1, 1)
    count = jnp.where(row == cells - 1, 1.0, 0.5) * jnp.where((lane == width - 1) & (core == 1), 1.0, 0.5)
    return (mine + turned) * (count * count_x)


def inner_kernel(
    own_ref, mate_ref, _arrived, ends_ref, elem_ref, edge_part_ref, sums_ref, edge_mode_ref, image_mode_ref, image_last_ref, side_ref, early_ref,
    node_ref, mode_ref, part_ref, stress_part_ref,
):
    core = lax.axis_index("gy")
    cells, width = own_ref.shape[2:]
    tiles = cells // 8
    zeros = lambda *dims: jnp.zeros(dims, jnp.float32)
    node_ref[:, :, :, 0:8, :] = zeros(4, 3, 2, 8, width)
    for x in range(4):
        for ref, block in ((own_ref, core), (mate_ref, 1 - core)):
            for field in range(3):
                node_ref[x, field, block, 8 : 8 + cells, :] = ref[x, field]
                if x in (0, 3):
                    ends_ref[x // 3, field, block] = ref[x, field]
            elem_ref[x, block] = ref[x, 3]

    @pl.loop(0, 4)
    def _(x):
        for field in range(3):
            high, low = ([node_ref[x, field, block, at : at + cells, :] for block in range(2)] for at in (8, 7))
            store_modes(mode_ref, x, field, high, low)

    edge_mode_ref[...] = mode_ref[3 * core]
    part_ref[:, :, :, cells : cells + 8, :] = zeros(2, 12, 2, 8, width)
    stress_part_ref[:, :, :, cells : cells + 8, :] = zeros(2, 6, 2, 8, width)

    @pl.loop(0, 2 * tiles, unroll=True)
    def _(t):
        block, rows = t // tiles, pl.ds(pl.multiple_of((t % tiles) * 8, 8), 8)
        load = lambda x: [[mode_ref[x, 4 * f + k, block, rows, :] for k in range(4)] for f in range(3)]
        low, kept, outer = load(0), None, None
        for x in range(1, 4):
            high = load(x)
            upper, lower = face_forces(mode_forces(element_modes(low, high), elem_ref[x, block, rows, :]))
            if kept is None:
                outer = lower
            else:
                for f, modes in enumerate(plus(kept, lower)):
                    for k, value in enumerate(corner_forces(modes)):
                        part_ref[x - 2, 4 * f + k, block, rows, :] = value
            low, kept = high, upper
        for f in range(3):
            for k in range(4):
                edge_part_ref[4 * f + k, block, rows, :] = jnp.where(core == 0, outer[f][k], kept[f][k])

    @pl.loop(0, 2 * tiles, unroll=True)
    def _(t):
        block, rows = t // tiles, pl.ds(pl.multiple_of((t % tiles) * 8, 8), 8)
        load = lambda x: [[mode_ref[x, 4 * f + k, block, rows, :] for k in range(3)] for f in range(3)]
        low, kept = load(0), None
        for x in range(1, 4):
            high = load(x)
            now = mode_stress(low, high, elem_ref[x, block, rows, :])
            for k in range(6):
                if x > 1:
                    stress_part_ref[x - 2, k, block, rows, :] = kept[k] + now[k]
                if x != 2:
                    side_ref[x // 2, k, block, rows, :] = now[k]
            low, kept = high, now

    fold = lambda value: value.reshape(tiles, 8, width).sum(0)
    norm = cross = square = zeros(8, width)
    for i in range(2):
        mine = jnp.where(core == i, 1.0, 0.0)
        for f in range(3):
            values = assembled(part_ref, i, f, cells)
            store_modes(image_mode_ref, i, f, values, last_ref=image_last_ref)
            early_ref[i, 6 + f] = jnp.where(core == 0, values[0], values[1])
            early_ref[i, 9 + f] = own_ref[1 + i, f]
            for block, value in enumerate(values):
                force = node_ref[i + 1, f, block, 8 : 8 + cells, :]
                norm = norm + mine * fold(force * force)
                cross = cross + mine * fold(force * value)
                square = square + mine * fold(value * value)
        for k in range(6):
            early_ref[i, k] = nodal_average(stress_part_ref, i, k, core, 0.5)
    for k, value in enumerate((norm, cross, square)):
        sums_ref[k] = value


def outer_kernel(
    ends_ref, elem_ref, edge_part_ref, part_sums_ref, edge_mode_ref, image_mode_ref, image_last_ref, same_ref, cross_ref,
    give_ref, sums_ref, halo_mode_ref, face_mode_ref, part_ref, halo_elem_ref,
):
    core, slab = lax.axis_index("gy"), lax.axis_index("gx")
    cells, width = same_ref.shape[2:]
    tiles = cells // 8
    zeros = lambda *dims: jnp.zeros(dims, jnp.float32)
    near = 1 - core
    first_core = core == 0
    for i in range(2):
        for f in range(4):
            same, cross = same_ref[i, f], cross_ref[i, f]
            values = [jnp.where(first_core, same, cross), jnp.where(first_core, cross, same)]
            if f < 3:
                store_modes(halo_mode_ref, i, f, values)
            else:
                halo_elem_ref[i, 0], halo_elem_ref[i, 1] = values
    for f in range(4):
        give_ref[6 + f, core] = same_ref[near, f]
        give_ref[6 + f, near] = cross_ref[near, f]

    part_ref[:, :, :, cells : cells + 8, :] = zeros(2, 12, 2, 8, width)

    @pl.loop(0, 2 * tiles, unroll=True)
    def _(t):
        block, rows = t // tiles, pl.ds(pl.multiple_of((t % tiles) * 8, 8), 8)
        load = lambda at: [[halo_mode_ref[at, 4 * f + k, block, rows, :] for k in range(4)] for f in range(3)]
        edge = [[edge_mode_ref[4 * f + k, block, rows, :] for k in range(4)] for f in range(3)]
        halo = [load(0), load(1)]
        planes = [pick(first_core, halo[0], edge), pick(first_core, halo[1], halo[0]), pick(first_core, edge, halo[1])]
        first = halo_elem_ref[near, block, rows, :]
        second = jnp.where(first_core, elem_ref[0, block, rows, :], halo_elem_ref[1, block, rows, :])
        upper, lower = face_forces(mode_forces(element_modes(planes[0], planes[1]), first))
        upper2, lower2 = face_forces(mode_forces(element_modes(planes[1], planes[2]), second))
        for f, modes in enumerate(plus(upper, lower2)):
            for k, value in enumerate(corner_forces(modes)):
                part_ref[0, 4 * f + k, block, rows, :] = value
        for f in range(3):
            modes = [edge_part_ref[4 * f + k, block, rows, :] + jnp.where(first_core, upper2[f][k], lower[f][k]) for k in range(4)]
            for k, value in enumerate(corner_forces(modes)):
                part_ref[1, 4 * f + k, block, rows, :] = value

    clamped = jnp.where(first_core & (slab == 0), 0.0, 1.0)
    fold = lambda value: value.reshape(tiles, 8, width).sum(0)
    norm, cross, square = (part_sums_ref[k] for k in range(3))
    for f in range(3):
        values = [value * clamped for value in assembled(part_ref, 0, f, cells)]
        store_modes(face_mode_ref, 0, f, values)
        for block in range(2):
            give_ref[f, block] = values[block]
        values = assembled(part_ref, 1, f, cells)
        store_modes(face_mode_ref, 1, f, values)
        for block, value in enumerate(values):
            give_ref[3 + f, block] = value
            force = ends_ref[core, f, block]
            norm = norm + fold(force * force)
            cross = cross + fold(force * value)
            square = square + fold(value * value)

    def energy_of(t, total):
        block, rows = t // tiles, pl.ds(pl.multiple_of((t % tiles) * 8, 8), 8)
        load = lambda ref, at: [[ref[at, 4 * f + k, block, rows, :] for k in range(4)] for f in range(3)]
        inner, beyond = (
            [[image_mode_ref[at, 3 * f + k, block, rows, :] for k in range(3)] + [image_last_ref[at, f, block, rows, :]] for f in range(3)]
            for at in range(2)
        )
        face = load(face_mode_ref, 1)
        planes = [pick(first_core, load(face_mode_ref, 0), inner), pick(first_core, face, beyond), pick(first_core, inner, face)]
        low = planes[0]
        for x in range(2):
            high = planes[x + 1]
            total = total + mode_energy(element_modes(low, high), elem_ref[2 * core + x, block, rows, :])
            low = high
        return total

    energy = lax.fori_loop(0, 2 * tiles, energy_of, zeros(8, width), unroll=True)
    packed = jnp.zeros((8, width), jnp.float32)
    for k, value in enumerate((norm, cross, square, energy)):
        value = value + pltpu.roll(value, width // 2, 1)
        value = value + pltpu.roll(value, width // 4, 1)
        packed = jnp.where(lanes((8, width)) // (width // 4) == k, value, packed)
    packed = jnp.sum(packed, axis=0, keepdims=True)
    sums_ref[...] = jnp.broadcast_to(packed[None], sums_ref.shape)


def stress_kernel(
    ends_ref, elem_ref, image_mode_ref, side_ref, give_ref, take_ref,
    late_ref, middle_ref, outer_mode_ref, face_mode_ref, part_ref, image_part_ref,
):
    core, slab = lax.axis_index("gy"), lax.axis_index("gx")
    cells, width = elem_ref.shape[2:]
    tiles = cells // 8
    count_last = jnp.where(slab == lax.axis_size("gx") - 1, 1.0, 0.5)
    zeros = lambda *dims: jnp.zeros(dims, jnp.float32)
    part_ref[:, :, :, cells : cells + 8, :] = zeros(2, 6, 2, 8, width)
    image_part_ref[:, :, :, cells : cells + 8, :] = zeros(4, 6, 2, 8, width)
    for f in range(3):
        for ref, mine in ((give_ref, core), (take_ref, 1 - core)):
            blocks = lambda base: [ref[base + f, block] for block in range(2)]
            store_modes(face_mode_ref, 3 * mine, f, blocks(0))
            store_modes(face_mode_ref, 1 + mine, f, blocks(3))
            store_modes(outer_mode_ref, 3 * mine, f, blocks(6))
        for i in range(2):
            store_modes(outer_mode_ref, 1 + i, f, [ends_ref[i, f, block] for block in range(2)])

    @pl.loop(0, 2 * tiles, unroll=True)
    def _(t):
        block, rows = t // tiles, pl.ds(pl.multiple_of((t % tiles) * 8, 8), 8)
        load = lambda ref, at, step=4: [[ref[at, step * f + k, block, rows, :] for k in range(3)] for f in range(3)]
        given, taken = give_ref[9, block, rows, :], take_ref[9, block, rows, :]
        modulus = [elem_ref[x, block, rows, :] for x in range(4)] + [jnp.where(core == 0, taken, given)]
        lower = mode_stress(load(outer_mode_ref, 0), load(outer_mode_ref, 1), modulus[0])
        upper = mode_stress(load(outer_mode_ref, 2), load(outer_mode_ref, 3), modulus[4])
        for k in range(6):
            part_ref[0, k, block, rows, :] = lower[k] + side_ref[0, k, block, rows, :]
            part_ref[1, k, block, rows, :] = side_ref[1, k, block, rows, :] + upper[k]
        planes = [(face_mode_ref, 0), (face_mode_ref, 1), (image_mode_ref, 0, 3), (image_mode_ref, 1, 3), (face_mode_ref, 2), (face_mode_ref, 3)]
        low, kept = load(*planes[0]), None
        for x in range(1, 6):
            high = load(*planes[x])
            now = mode_stress(low, high, modulus[x - 1])
            if kept is not None:
                for k in range(6):
                    image_part_ref[x - 2, k, block, rows, :] = kept[k] + now[k]
            low, kept = high, now

    for i in range(2):
        count = count_last if i else 0.5
        for k in range(6):
            late_ref[i, k] = nodal_average(part_ref, i, k, core, count)
            late_ref[i, 12 + k] = nodal_average(image_part_ref, 3 * i, k, core, count)
            middle_ref[i, k] = nodal_average(image_part_ref, 1 + i, k, core, 0.5)
        for f in range(3):
            late_ref[i, 6 + f] = jnp.where(core == i, give_ref[3 + f, core], take_ref[3 + f, core])
            late_ref[i, 9 + f] = ends_ref[i, f, core]


def combine_kernel(sums_ref, early_ref, late_ref, middle_ref, field_ref, stress_ref):
    total = jnp.sum(sums_ref[...], axis=0)
    quarter = lanes(total.shape) // (total.shape[1] // 4)
    norm, cross, square, energy = (jnp.sum(jnp.where(quarter == k, total, 0.0), axis=1, keepdims=True) for k in range(4))
    first = norm / cross
    norm_next = norm - 2.0 * first * cross + first * first * square
    ratio = norm_next / norm
    grown = 1.0 + ratio
    curvature = grown * grown * cross - 2.0 * grown * first * square + first * first * energy
    second = norm_next / curvature
    weight = jnp.broadcast_to(first + second * grown, early_ref.shape[2:])
    weight_image = jnp.broadcast_to(-second * first, early_ref.shape[2:])
    cells = early_ref.shape[2]
    for x in range(4):
        rows, i = pl.ds(x, cells, stride=4), (0, 0, 1, 1)[x]
        first_ref = late_ref if x in (0, 3) else early_ref
        for f in range(3):
            field_ref[f, rows, :] = weight * first_ref[i, 9 + f] + weight_image * first_ref[i, 6 + f]
        for k in range(6):
            image = late_ref[i, 12 + k] if x in (0, 3) else middle_ref[i, k]
            stress_ref[k, rows, :] = weight * first_ref[i, k] + weight_image * image


def cost(flops, size):
    return pl.CostEstimate(flops=flops, bytes_accessed=size, transcendentals=0)


def per_device(body_force, modulus):
    cells, planes, width = modulus.shape
    slabs, cores = lax.axis_size("gx"), lax.axis_size("gy")
    assert planes == 4 and cores == 2 and cells % 8 == 0
    both = ("gx", "gy")
    f32 = jnp.float32
    shape = lambda *dims: jax.ShapeDtypeStruct(dims, f32)
    scratch = lambda *dims: pltpu.VMEM(dims, f32)

    own, same, cross = pl.pallas_call(
        pack_kernel,
        out_shape=(shape(4, 4, cells, width), shape(2, 4, cells, width), shape(2, 4, cells, width)),
        in_specs=[pl.BlockSpec(memory_space=pl.ANY)] * 2,
        out_specs=[VMEM] * 3,
        scratch_shapes=[scratch(3, cells * 4, width), scratch(cells * 4, width), pltpu.SemaphoreType.DMA((2,))],
        compiler_params=LIMIT,
        name="pack",
    )(
        pltpu.with_memory_space_constraint(body_force.reshape(3, cells * 4, width), pltpu.HBM),
        pltpu.with_memory_space_constraint(modulus.reshape(cells * 4, width), pltpu.HBM),
    )

    up = [(2 * g, 2 * g + 2) for g in range(slabs - 1)]
    down = [(2 * g + 3, 2 * g + 1) for g in range(slabs - 1)]
    pairs = [(2 * g + 1, 2 * g + 2) for g in range(slabs - 1)]
    mate = lax.ppermute(own, "gy", [(0, 1), (1, 0)])
    cross_in = lax.ppermute(cross, both, pairs + [(q, p) for p, q in pairs])
    same_in = lax.ppermute(same, both, up + down)

    ends, elem, edge_part, part_sums, edge_mode, image_mode, image_last, side, early = pl.pallas_call(
        inner_kernel,
        out_shape=(
            shape(2, 3, 2, cells, width),
            shape(4, 2, cells, width),
            shape(12, 2, cells, width),
            shape(3, 8, width),
            shape(12, 2, cells, width),
            shape(2, 9, 2, cells, width),
            shape(2, 3, 2, cells, width),
            shape(2, 6, 2, cells, width),
            shape(2, 12, cells, width),
        ),
        in_specs=[VMEM] * 2 + [pl.BlockSpec(memory_space=pl.ANY)],
        out_specs=[VMEM] * 9,
        scratch_shapes=[
            scratch(4, 3, 2, 8 + cells, width),
            scratch(4, 12, 2, cells, width),
            scratch(2, 12, 2, 8 + cells, width),
            scratch(2, 6, 2, 8 + cells, width),
        ],
        compiler_params=LIMIT,
        cost_estimate=cost(20_000_000, 4_000_000),
        name="inner",
    )(own, mate, cross_in)
    give, sums = pl.pallas_call(
        outer_kernel,
        out_shape=(shape(10, 2, cells, width), shape(slabs * cores, 1, width)),
        in_specs=[VMEM] * 9,
        out_specs=[VMEM] * 2,
        scratch_shapes=[
            scratch(2, 12, 2, cells, width),
            scratch(2, 12, 2, cells, width),
            scratch(2, 12, 2, 8 + cells, width),
            scratch(2, 2, cells, width),
        ],
        compiler_params=LIMIT,
        cost_estimate=cost(10_000_000, 3_000_000),
        name="outer",
    )(ends, elem, edge_part, part_sums, edge_mode, image_mode, image_last, same_in, cross_in)

    take = lax.ppermute(give, "gy", [(0, 1), (1, 0)])
    sums = lax.all_to_all(sums, both, 0, 0, axis_index_groups=[list(range(slabs * cores))[::-1]])
    late, middle = pl.pallas_call(
        stress_kernel,
        out_shape=(shape(2, 18, cells, width), shape(2, 6, cells, width)),
        in_specs=[VMEM] * 6,
        out_specs=[VMEM] * 2,
        scratch_shapes=[
            scratch(4, 12, 2, cells, width),
            scratch(4, 12, 2, cells, width),
            scratch(2, 6, 2, 8 + cells, width),
            scratch(4, 6, 2, 8 + cells, width),
        ],
        compiler_params=LIMIT,
        cost_estimate=cost(20_000_000, 4_000_000),
        name="stress",
    )(ends, elem, image_mode, side, give, take)

    field, stress = pl.pallas_call(
        combine_kernel,
        out_shape=(shape(3, cells * 4, width), shape(6, cells * 4, width)),
        in_specs=[VMEM] * 4,
        out_specs=[VMEM] * 2,
        compiler_params=LIMIT,
        name="combine",
    )(sums, early, late, middle)
    return field.reshape(3, cells, 4, width), stress.reshape(6, cells, 4, width)


def solution(mesh):
    return jax.shard_map(
        per_device,
        mesh=mesh,
        in_specs=(P(None, "sample", "gx", "gy"), P("sample", "gx", "gy")),
        out_specs=(P(None, "sample", "gx", "gy"), P(None, "sample", "gx", "gy")),
        check_vma=False,
    )
```

```python
import functools

import jax
import jax.numpy as jnp
from jax import lax
from jax.experimental import pallas as pl
from jax.experimental.pallas import tpu as pltpu
from jax.sharding import PartitionSpec as P

POISSON = 0.3
LAME = POISSON / ((1.0 + POISSON) * (1.0 - 2.0 * POISSON))
SHEAR = 1.0 / (2.0 * (1.0 + POISSON))
RATIO = LAME / SHEAR
ONE = SHEAR / 16.0
TWO = SHEAR / 48.0
THREE = (LAME + 4.0 * SHEAR) / 144.0

VMEM = pl.BlockSpec(memory_space=pltpu.VMEM)
LIMIT = pltpu.CompilerParams(vmem_limit_bytes=48 << 20)


def lanes(shape):
    return lax.broadcasted_iota(jnp.int32, shape, len(shape) - 1)


def from_left(first, second):
    edge = lanes(first.shape) == 0
    turned, turned2 = pltpu.roll(first, 1, 1), pltpu.roll(second, 1, 1)
    return jnp.where(edge, 0.0, turned), jnp.where(edge, turned, turned2)


def from_right(first, second):
    edge = lanes(first.shape) == first.shape[1] - 1
    turned, turned2 = (pltpu.roll(v, v.shape[1] - 1, 1) for v in (first, second))
    return jnp.where(edge, turned2, turned), jnp.where(edge, 0.0, turned2)


def pack_kernel(force_hbm, modulus_hbm, own_ref, same_ref, cross_ref, force_ref, modulus_ref, sem):
    core = lax.axis_index("gy")
    cells = own_ref.shape[2]
    copies = [pltpu.make_async_copy(force_hbm.at[field], force_ref.at[field], sem.at[field]) for field in range(3)]
    copies.append(pltpu.make_async_copy(modulus_hbm, modulus_ref, sem.at[3]))
    for copy in copies:
        copy.start()

    def plane(field, x):
        rows = pl.ds(x, cells, stride=4)
        return force_ref[field, rows, :] if field < 3 else modulus_ref[rows, :]

    for field in range(4):
        copies[field].wait()
        for x in range(4):
            own_ref[x, field] = plane(field, x)
        for i in range(2):
            same_ref[i, field] = plane(field, 2 * (1 - core) + i)
            cross_ref[i, field] = plane(field, 2 * core + i)


def below(value):
    row = lax.broadcasted_iota(jnp.int32, value.shape, 0)
    return jnp.where(row == 0, 0.0, pltpu.roll(value, 1, 0))


def store_modes(mode_ref, at, field, high, low=None, last_ref=None):
    base = 4 * field if last_ref is None else 3 * field
    left = from_left(*high)
    for block in range(2):
        value, beside = high[block], left[block]
        value_low = below(value) if low is None else low[block]
        beside_low = below(beside)
        total, total_beside = value + value_low, beside + beside_low
        slope, slope_beside = value - value_low, beside - beside_low
        mode_ref[at, base, block] = total + total_beside
        mode_ref[at, base + 1, block] = slope + slope_beside
        mode_ref[at, base + 2, block] = total - total_beside
        if last_ref is None:
            mode_ref[at, base + 3, block] = slope - slope_beside
        else:
            last_ref[at, field, block] = slope - slope_beside


def element_modes(low, high):
    found = []
    for component in range(3):
        modes = {}
        for kind, (z, y) in enumerate(((0, 0), (1, 0), (0, 1), (1, 1))):
            lo, hi = low[component][kind], high[component][kind]
            if (z, y) != (0, 0):
                modes[z, 0, y] = hi + lo
            modes[z, 1, y] = hi - lo
        found.append(modes)
    return found


def mode_forces(modes, modulus):
    u, v, w = modes
    one, two, three = modulus * ONE, modulus * TWO, modulus * THREE
    trace = RATIO * (u[1, 0, 0] + v[0, 1, 0] + w[0, 0, 1])
    shear_zx = one * (u[0, 1, 0] + v[1, 0, 0])
    shear_xy = one * (v[0, 0, 1] + w[0, 1, 0])
    shear_zy = one * (u[0, 0, 1] + w[1, 0, 0])
    trace_z = RATIO * (v[1, 1, 0] + w[1, 0, 1])
    trace_x = RATIO * (u[1, 1, 0] + w[0, 1, 1])
    trace_y = RATIO * (u[1, 0, 1] + v[0, 1, 1])
    mixed_zx = u[0, 1, 1] + v[1, 0, 1]
    mixed_xy = v[1, 0, 1] + w[1, 1, 0]
    mixed_zy = u[0, 1, 1] + w[1, 1, 0]
    return (
        {
            (1, 0, 0): one * (trace + 2.0 * u[1, 0, 0]),
            (0, 1, 0): shear_zx,
            (0, 0, 1): shear_zy,
            (1, 1, 0): two * (trace_x + 3.0 * u[1, 1, 0]),
            (1, 0, 1): two * (trace_y + 3.0 * u[1, 0, 1]),
            (0, 1, 1): two * (mixed_zx + mixed_zy),
            (1, 1, 1): three * u[1, 1, 1],
        },
        {
            (0, 1, 0): one * (trace + 2.0 * v[0, 1, 0]),
            (1, 0, 0): shear_zx,
            (0, 0, 1): shear_xy,
            (1, 1, 0): two * (trace_z + 3.0 * v[1, 1, 0]),
            (0, 1, 1): two * (trace_y + 3.0 * v[0, 1, 1]),
            (1, 0, 1): two * (mixed_zx + mixed_xy),
            (1, 1, 1): three * v[1, 1, 1],
        },
        {
            (0, 0, 1): one * (trace + 2.0 * w[0, 0, 1]),
            (1, 0, 0): shear_zy,
            (0, 1, 0): shear_xy,
            (1, 0, 1): two * (trace_z + 3.0 * w[1, 0, 1]),
            (0, 1, 1): two * (trace_x + 3.0 * w[0, 1, 1]),
            (1, 1, 0): two * (mixed_xy + mixed_zy),
            (1, 1, 1): three * w[1, 1, 1],
        },
    )


def mode_energy(modes, modulus):
    u, v, w = modes
    square = lambda value: value * value
    a, b, c = u[1, 0, 0], v[0, 1, 0], w[0, 0, 1]
    one = RATIO * square(a + b + c) + 2.0 * (square(a) + square(b) + square(c))
    one = one + square(u[0, 1, 0] + v[1, 0, 0]) + square(v[0, 0, 1] + w[0, 1, 0]) + square(u[0, 0, 1] + w[1, 0, 0])
    d, e, f = u[1, 1, 0], u[1, 0, 1], v[1, 1, 0]
    g, h, k = v[0, 1, 1], w[1, 0, 1], w[0, 1, 1]
    two = RATIO * (square(f + h) + square(d + k) + square(e + g))
    two = two + 3.0 * (square(d) + square(e) + square(f) + square(g) + square(h) + square(k))
    m, n, o = u[0, 1, 1], v[1, 0, 1], w[1, 1, 0]
    two = two + square(m + n) + square(n + o) + square(m + o)
    three = square(u[1, 1, 1]) + square(v[1, 1, 1]) + square(w[1, 1, 1])
    return modulus * (ONE * one + TWO * two + THREE * three)


def face_forces(forces):
    upper, lower = [], []
    for component in range(3):
        up, down = [], []
        for z, y in ((0, 0), (1, 0), (0, 1), (1, 1)):
            diff, both = forces[component][z, 1, y], forces[component].get((z, 0, y))
            up.append(diff if both is None else both + diff)
            down.append(-diff if both is None else both - diff)
        upper.append(up)
        lower.append(down)
    return upper, lower


def corner_forces(modes):
    ss, ds, sd, dd = modes
    here, back = ss + ds, ss - ds
    here_y, back_y = sd + dd, sd - dd
    return here + here_y, here - here_y, back + back_y, back - back_y


def plus(first, second):
    return [[p + q for p, q in zip(a, b)] for a, b in zip(first, second)]


def pick(flag, first, second):
    return [[jnp.where(flag, p, q) for p, q in zip(a, b)] for a, b in zip(first, second)]


def assembled(part_ref, at, field, cells):
    here = lambda k, block: part_ref[at, 4 * field + k, block, 0:cells, :]
    above = lambda k, block: part_ref[at, 4 * field + k, block, 1 : cells + 1, :]
    beside = from_right(*(here(1, block) + above(3, block) for block in range(2)))
    return [here(0, block) + above(2, block) + beside[block] for block in range(2)]


def mode_stress(low, high, modulus):
    by_z = [high[f][1] + low[f][1] for f in range(3)]
    by_x = [high[f][0] - low[f][0] for f in range(3)]
    by_y = [high[f][2] + low[f][2] for f in range(3)]
    scaled = modulus * (0.25 * SHEAR)
    trace = RATIO * (by_z[0] + by_x[1] + by_y[2])
    return [
        scaled * (trace + 2.0 * by_z[0]),
        scaled * (trace + 2.0 * by_x[1]),
        scaled * (trace + 2.0 * by_y[2]),
        scaled * (by_x[0] + by_z[1]),
        scaled * (by_y[1] + by_x[2]),
        scaled * (by_y[0] + by_z[2]),
    ]


def nodal_average(part_ref, at, k, core, count_x):
    cells, width = part_ref.shape[3] - 8, part_ref.shape[4]
    both = [part_ref[at, k, block, 0:cells, :] + part_ref[at, k, block, 1 : cells + 1, :] for block in range(2)]
    first, second = both
    lane = lanes((cells, width))
    row = lax.broadcasted_iota(jnp.int32, (cells, width), 0)
    mine = jnp.where(core == 0, first, second)
    turned = pltpu.roll(jnp.where(lane == 0, jnp.where(core == 0, second, 0.0), mine), width - 1, 1)
    count = jnp.where(row == cells - 1, 1.0, 0.5) * jnp.where((lane == width - 1) & (core == 1), 1.0, 0.5)
    return (mine + turned) * (count * count_x)


def inner_kernel(
    own_ref, mate_ref, _arrived, ends_ref, elem_ref, edge_part_ref, sums_ref, edge_mode_ref, image_mode_ref, image_last_ref, side_ref, early_ref,
    node_ref, mode_ref, part_ref, stress_part_ref,
):
    core = lax.axis_index("gy")
    cells, width = own_ref.shape[2:]
    tiles = cells // 8
    zeros = lambda *dims: jnp.zeros(dims, jnp.float32)
    node_ref[:, :, :, 0:8, :] = zeros(4, 3, 2, 8, width)
    for x in range(4):
        for ref, block in ((own_ref, core), (mate_ref, 1 - core)):
            for field in range(3):
                node_ref[x, field, block, 8 : 8 + cells, :] = ref[x, field]
                if x in (0, 3):
                    ends_ref[x // 3, field, block] = ref[x, field]
            elem_ref[x, block] = ref[x, 3]

    @pl.loop(0, 4)
    def _(x):
        for field in range(3):
            high, low = ([node_ref[x, field, block, at : at + cells, :] for block in range(2)] for at in (8, 7))
            store_modes(mode_ref, x, field, high, low)

    edge_mode_ref[...] = mode_ref[3 * core]
    part_ref[:, :, :, cells : cells + 8, :] = zeros(2, 12, 2, 8, width)
    stress_part_ref[:, :, :, cells : cells + 8, :] = zeros(2, 6, 2, 8, width)

    @pl.loop(0, 2 * tiles, unroll=True)
    def _(t):
        block, rows = t // tiles, pl.ds(pl.multiple_of((t % tiles) * 8, 8), 8)
        load = lambda x: [[mode_ref[x, 4 * f + k, block, rows, :] for k in range(4)] for f in range(3)]
        low, kept, outer = load(0), None, None
        for x in range(1, 4):
            high = load(x)
            upper, lower = face_forces(mode_forces(element_modes(low, high), elem_ref[x, block, rows, :]))
            if kept is None:
                outer = lower
            else:
                for f, modes in enumerate(plus(kept, lower)):
                    for k, value in enumerate(corner_forces(modes)):
                        part_ref[x - 2, 4 * f + k, block, rows, :] = value
            low, kept = high, upper
        for f in range(3):
            for k in range(4):
                edge_part_ref[4 * f + k, block, rows, :] = jnp.where(core == 0, outer[f][k], kept[f][k])

    @pl.loop(0, 2 * tiles, unroll=True)
    def _(t):
        block, rows = t // tiles, pl.ds(pl.multiple_of((t % tiles) * 8, 8), 8)
        load = lambda x: [[mode_ref[x, 4 * f + k, block, rows, :] for k in range(3)] for f in range(3)]
        low, kept = load(0), None
        for x in range(1, 4):
            high = load(x)
            now = mode_stress(low, high, elem_ref[x, block, rows, :])
            for k in range(6):
                if x > 1:
                    stress_part_ref[x - 2, k, block, rows, :] = kept[k] + now[k]
                if x != 2:
                    side_ref[x // 2, k, block, rows, :] = now[k]
            low, kept = high, now

    fold = lambda value: value.reshape(tiles, 8, width).sum(0)
    norm = cross = square = zeros(8, width)
    for i in range(2):
        mine = jnp.where(core == i, 1.0, 0.0)
        for f in range(3):
            values = assembled(part_ref, i, f, cells)
            store_modes(image_mode_ref, i, f, values, last_ref=image_last_ref)
            early_ref[i, 6 + f] = jnp.where(core == 0, values[0], values[1])
            early_ref[i, 9 + f] = own_ref[1 + i, f]
            for block, value in enumerate(values):
                force = node_ref[i + 1, f, block, 8 : 8 + cells, :]
                norm = norm + mine * fold(force * force)
                cross = cross + mine * fold(force * value)
                square = square + mine * fold(value * value)
        for k in range(6):
            early_ref[i, k] = nodal_average(stress_part_ref, i, k, core, 0.5)
    for k, value in enumerate((norm, cross, square)):
        sums_ref[k] = value


def outer_kernel(
    ends_ref, elem_ref, edge_part_ref, part_sums_ref, edge_mode_ref, image_mode_ref, image_last_ref, same_ref, cross_ref,
    give_ref, sums_ref, halo_mode_ref, face_mode_ref, part_ref, halo_elem_ref,
):
    core, slab = lax.axis_index("gy"), lax.axis_index("gx")
    cells, width = same_ref.shape[2:]
    tiles = cells // 8
    zeros = lambda *dims: jnp.zeros(dims, jnp.float32)
    near = 1 - core
    first_core = core == 0
    for i in range(2):
        for f in range(4):
            same, cross = same_ref[i, f], cross_ref[i, f]
            values = [jnp.where(first_core, same, cross), jnp.where(first_core, cross, same)]
            if f < 3:
                store_modes(halo_mode_ref, i, f, values)
            else:
                halo_elem_ref[i, 0], halo_elem_ref[i, 1] = values
    for f in range(4):
        give_ref[6 + f, core] = same_ref[near, f]
        give_ref[6 + f, near] = cross_ref[near, f]

    part_ref[:, :, :, cells : cells + 8, :] = zeros(2, 12, 2, 8, width)

    @pl.loop(0, 2 * tiles, unroll=True)
    def _(t):
        block, rows = t // tiles, pl.ds(pl.multiple_of((t % tiles) * 8, 8), 8)
        load = lambda at: [[halo_mode_ref[at, 4 * f + k, block, rows, :] for k in range(4)] for f in range(3)]
        edge = [[edge_mode_ref[4 * f + k, block, rows, :] for k in range(4)] for f in range(3)]
        halo = [load(0), load(1)]
        planes = [pick(first_core, halo[0], edge), pick(first_core, halo[1], halo[0]), pick(first_core, edge, halo[1])]
        first = halo_elem_ref[near, block, rows, :]
        second = jnp.where(first_core, elem_ref[0, block, rows, :], halo_elem_ref[1, block, rows, :])
        upper, lower = face_forces(mode_forces(element_modes(planes[0], planes[1]), first))
        upper2, lower2 = face_forces(mode_forces(element_modes(planes[1], planes[2]), second))
        for f, modes in enumerate(plus(upper, lower2)):
            for k, value in enumerate(corner_forces(modes)):
                part_ref[0, 4 * f + k, block, rows, :] = value
        for f in range(3):
            modes = [edge_part_ref[4 * f + k, block, rows, :] + jnp.where(first_core, upper2[f][k], lower[f][k]) for k in range(4)]
            for k, value in enumerate(corner_forces(modes)):
                part_ref[1, 4 * f + k, block, rows, :] = value

    clamped = jnp.where(first_core & (slab == 0), 0.0, 1.0)
    fold = lambda value: value.reshape(tiles, 8, width).sum(0)
    norm, cross, square = (part_sums_ref[k] for k in range(3))
    for f in range(3):
        values = [value * clamped for value in assembled(part_ref, 0, f, cells)]
        store_modes(face_mode_ref, 0, f, values)
        for block in range(2):
            give_ref[f, block] = values[block]
        values = assembled(part_ref, 1, f, cells)
        store_modes(face_mode_ref, 1, f, values)
        for block, value in enumerate(values):
            give_ref[3 + f, block] = value
            force = ends_ref[core, f, block]
            norm = norm + fold(force * force)
            cross = cross + fold(force * value)
            square = square + fold(value * value)

    def energy_of(t, total):
        block, rows = t // tiles, pl.ds(pl.multiple_of((t % tiles) * 8, 8), 8)
        load = lambda ref, at: [[ref[at, 4 * f + k, block, rows, :] for k in range(4)] for f in range(3)]
        inner, beyond = (
            [[image_mode_ref[at, 3 * f + k, block, rows, :] for k in range(3)] + [image_last_ref[at, f, block, rows, :]] for f in range(3)]
            for at in range(2)
        )
        face = load(face_mode_ref, 1)
        planes = [pick(first_core, load(face_mode_ref, 0), inner), pick(first_core, face, beyond), pick(first_core, inner, face)]
        low = planes[0]
        for x in range(2):
            high = planes[x + 1]
            total = total + mode_energy(element_modes(low, high), elem_ref[2 * core + x, block, rows, :])
            low = high
        return total

    energy = lax.fori_loop(0, 2 * tiles, energy_of, zeros(8, width), unroll=True)
    packed = jnp.zeros((8, width), jnp.float32)
    for k, value in enumerate((norm, cross, square, energy)):
        value = value + pltpu.roll(value, width // 2, 1)
        value = value + pltpu.roll(value, width // 4, 1)
        packed = jnp.where(lanes((8, width)) // (width // 4) == k, value, packed)
    packed = jnp.sum(packed, axis=0, keepdims=True)
    sums_ref[...] = jnp.broadcast_to(packed[None], sums_ref.shape)


def stress_kernel(
    ends_ref, elem_ref, image_mode_ref, side_ref, give_ref, take_ref,
    late_ref, middle_ref, outer_mode_ref, face_mode_ref, part_ref, image_part_ref,
):
    core, slab = lax.axis_index("gy"), lax.axis_index("gx")
    cells, width = elem_ref.shape[2:]
    tiles = cells // 8
    count_last = jnp.where(slab == lax.axis_size("gx") - 1, 1.0, 0.5)
    zeros = lambda *dims: jnp.zeros(dims, jnp.float32)
    part_ref[:, :, :, cells : cells + 8, :] = zeros(2, 6, 2, 8, width)
    image_part_ref[:, :, :, cells : cells + 8, :] = zeros(4, 6, 2, 8, width)
    for f in range(3):
        for ref, mine in ((give_ref, core), (take_ref, 1 - core)):
            blocks = lambda base: [ref[base + f, block] for block in range(2)]
            store_modes(face_mode_ref, 3 * mine, f, blocks(0))
            store_modes(face_mode_ref, 1 + mine, f, blocks(3))
            store_modes(outer_mode_ref, 3 * mine, f, blocks(6))
        for i in range(2):
            store_modes(outer_mode_ref, 1 + i, f, [ends_ref[i, f, block] for block in range(2)])

    @pl.loop(0, 2 * tiles, unroll=True)
    def _(t):
        block, rows = t // tiles, pl.ds(pl.multiple_of((t % tiles) * 8, 8), 8)
        load = lambda ref, at, step=4: [[ref[at, step * f + k, block, rows, :] for k in range(3)] for f in range(3)]
        given, taken = give_ref[9, block, rows, :], take_ref[9, block, rows, :]
        modulus = [elem_ref[x, block, rows, :] for x in range(4)] + [jnp.where(core == 0, taken, given)]
        lower = mode_stress(load(outer_mode_ref, 0), load(outer_mode_ref, 1), modulus[0])
        upper = mode_stress(load(outer_mode_ref, 2), load(outer_mode_ref, 3), modulus[4])
        for k in range(6):
            part_ref[0, k, block, rows, :] = lower[k] + side_ref[0, k, block, rows, :]
            part_ref[1, k, block, rows, :] = side_ref[1, k, block, rows, :] + upper[k]
        planes = [(face_mode_ref, 0), (face_mode_ref, 1), (image_mode_ref, 0, 3), (image_mode_ref, 1, 3), (face_mode_ref, 2), (face_mode_ref, 3)]
        low, kept = load(*planes[0]), None
        for x in range(1, 6):
            high = load(*planes[x])
            now = mode_stress(low, high, modulus[x - 1])
            if kept is not None:
                for k in range(6):
                    image_part_ref[x - 2, k, block, rows, :] = kept[k] + now[k]
            low, kept = high, now

    for i in range(2):
        count = count_last if i else 0.5
        for k in range(6):
            late_ref[i, k] = nodal_average(part_ref, i, k, core, count)
            late_ref[i, 12 + k] = nodal_average(image_part_ref, 3 * i, k, core, count)
            middle_ref[i, k] = nodal_average(image_part_ref, 1 + i, k, core, 0.5)
        for f in range(3):
            late_ref[i, 6 + f] = jnp.where(core == i, give_ref[3 + f, core], take_ref[3 + f, core])
            late_ref[i, 9 + f] = ends_ref[i, f, core]


def combine_kernel(sums_ref, early_ref, late_ref, middle_ref, field_ref, stress_ref):
    total = jnp.sum(sums_ref[...], axis=0)
    quarter = lanes(total.shape) // (total.shape[1] // 4)
    norm, cross, square, energy = (jnp.sum(jnp.where(quarter == k, total, 0.0), axis=1, keepdims=True) for k in range(4))
    first = norm / cross
    norm_next = norm - 2.0 * first * cross + first * first * square
    ratio = norm_next / norm
    grown = 1.0 + ratio
    curvature = grown * grown * cross - 2.0 * grown * first * square + first * first * energy
    second = norm_next / curvature
    weight = jnp.broadcast_to(first + second * grown, early_ref.shape[2:])
    weight_image = jnp.broadcast_to(-second * first, early_ref.shape[2:])
    cells = early_ref.shape[2]
    for x in range(4):
        rows, i = pl.ds(x, cells, stride=4), (0, 0, 1, 1)[x]
        first_ref = late_ref if x in (0, 3) else early_ref
        for f in range(3):
            field_ref[f, rows, :] = weight * first_ref[i, 9 + f] + weight_image * first_ref[i, 6 + f]
        for k in range(6):
            image = late_ref[i, 12 + k] if x in (0, 3) else middle_ref[i, k]
            stress_ref[k, rows, :] = weight * first_ref[i, k] + weight_image * image


def cost(flops, size):
    return pl.CostEstimate(flops=flops, bytes_accessed=size, transcendentals=0)


def per_device(body_force, modulus):
    cells, planes, width = modulus.shape
    slabs, cores = lax.axis_size("gx"), lax.axis_size("gy")
    assert planes == 4 and cores == 2 and cells % 8 == 0
    both = ("gx", "gy")
    f32 = jnp.float32
    shape = lambda *dims: jax.ShapeDtypeStruct(dims, f32)
    scratch = lambda *dims: pltpu.VMEM(dims, f32)

    own, same, cross = pl.pallas_call(
        pack_kernel,
        out_shape=(shape(4, 4, cells, width), shape(2, 4, cells, width), shape(2, 4, cells, width)),
        in_specs=[pl.BlockSpec(memory_space=pl.ANY)] * 2,
        out_specs=[VMEM] * 3,
        scratch_shapes=[scratch(3, cells * 4, width), scratch(cells * 4, width), pltpu.SemaphoreType.DMA((4,))],
        compiler_params=LIMIT,
        name="pack",
    )(
        pltpu.with_memory_space_constraint(body_force.reshape(3, cells * 4, width), pltpu.HBM),
        pltpu.with_memory_space_constraint(modulus.reshape(cells * 4, width), pltpu.HBM),
    )

    up = [(2 * g, 2 * g + 2) for g in range(slabs - 1)]
    down = [(2 * g + 3, 2 * g + 1) for g in range(slabs - 1)]
    pairs = [(2 * g + 1, 2 * g + 2) for g in range(slabs - 1)]
    mate = lax.ppermute(own, "gy", [(0, 1), (1, 0)])
    cross_in = lax.ppermute(cross, both, pairs + [(q, p) for p, q in pairs])
    same_in = lax.ppermute(same, both, up + down)

    ends, elem, edge_part, part_sums, edge_mode, image_mode, image_last, side, early = pl.pallas_call(
        inner_kernel,
        out_shape=(
            shape(2, 3, 2, cells, width),
            shape(4, 2, cells, width),
            shape(12, 2, cells, width),
            shape(3, 8, width),
            shape(12, 2, cells, width),
            shape(2, 9, 2, cells, width),
            shape(2, 3, 2, cells, width),
            shape(2, 6, 2, cells, width),
            shape(2, 12, cells, width),
        ),
        in_specs=[VMEM] * 2 + [pl.BlockSpec(memory_space=pl.ANY)],
        out_specs=[VMEM] * 9,
        scratch_shapes=[
            scratch(4, 3, 2, 8 + cells, width),
            scratch(4, 12, 2, cells, width),
            scratch(2, 12, 2, 8 + cells, width),
            scratch(2, 6, 2, 8 + cells, width),
        ],
        compiler_params=LIMIT,
        cost_estimate=cost(20_000_000, 4_000_000),
        name="inner",
    )(own, mate, cross_in)
    give, sums = pl.pallas_call(
        outer_kernel,
        out_shape=(shape(10, 2, cells, width), shape(slabs * cores, 1, width)),
        in_specs=[VMEM] * 9,
        out_specs=[VMEM] * 2,
        scratch_shapes=[
            scratch(2, 12, 2, cells, width),
            scratch(2, 12, 2, cells, width),
            scratch(2, 12, 2, 8 + cells, width),
            scratch(2, 2, cells, width),
        ],
        compiler_params=LIMIT,
        cost_estimate=cost(10_000_000, 3_000_000),
        name="outer",
    )(ends, elem, edge_part, part_sums, edge_mode, image_mode, image_last, same_in, cross_in)

    take = lax.ppermute(give, "gy", [(0, 1), (1, 0)])
    sums = lax.all_to_all(sums, both, 0, 0, axis_index_groups=[list(range(slabs * cores))[::-1]])
    late, middle = pl.pallas_call(
        stress_kernel,
        out_shape=(shape(2, 18, cells, width), shape(2, 6, cells, width)),
        in_specs=[VMEM] * 6,
        out_specs=[VMEM] * 2,
        scratch_shapes=[
            scratch(4, 12, 2, cells, width),
            scratch(4, 12, 2, cells, width),
            scratch(2, 6, 2, 8 + cells, width),
            scratch(4, 6, 2, 8 + cells, width),
        ],
        compiler_params=LIMIT,
        cost_estimate=cost(20_000_000, 4_000_000),
        name="stress",
    )(ends, elem, image_mode, side, give, take)

    field, stress = pl.pallas_call(
        combine_kernel,
        out_shape=(shape(3, cells * 4, width), shape(6, cells * 4, width)),
        in_specs=[VMEM] * 4,
        out_specs=[VMEM] * 2,
        compiler_params=LIMIT,
        name="combine",
    )(sums, early, late, middle)
    return field.reshape(3, cells, 4, width), stress.reshape(6, cells, 4, width)


def solution(mesh):
    return jax.shard_map(
        per_device,
        mesh=mesh,
        in_specs=(P(None, "sample", "gx", "gy"), P("sample", "gx", "gy")),
        out_specs=(P(None, "sample", "gx", "gy"), P(None, "sample", "gx", "gy")),
        check_vma=False,
    )
```
